768 devices in a mesh: ctx: 24 (over x_hi, z), exp: 32 (over y, x_lo, core).
Axes of the slice: x: 4 (x_hi: 2, x_lo: 2; x = x_hi * 2 + x_lo), y: 8, z: 12, core: 2. Of those that a mesh axis runs over, the one named last changes fastest.
Arguments:
- queries: bfloat16 [32, 1536, 1024], P('exp', 'ctx'), may hold values from -6 to 6
- keys: bfloat16 [32, 1536, 1024], P('exp', 'ctx'), may hold values from -6 to 6
- values: bfloat16 [32, 1536, 1024], P('exp', 'ctx'), may hold values from -6 to 6
- residual: bfloat16 [32, 1536, 2048], P('exp', 'ctx'), may hold values from -6 to 6
- out_proj: bfloat16 [1024, 2048], replicated, may hold values from -0.1875 to 0.1875
- norm_gain: float32 [2048], replicated, may hold values from 0.25 to 1.75
- w_gate: bfloat16 [32, 2048, 512], P('exp'), may hold values from -0.125 to 0.125
- w_up: bfloat16 [32, 2048, 512], P('exp'), may hold values from -0.125 to 0.125
- w_down: bfloat16 [32, 512, 2048], P('exp'), may hold values from -0.25 to 0.25
- routes: int32 [32, 1536, 4], P('exp', 'ctx'), may hold values from 0 to 31, all different within a row; in each aligned block of 64 rows (0 to 63, 64 to 127, ..., all dimensions but the last counted through in order) at most 12 rows name the same one
- route_prob: float32 [32, 1536, 4], P('exp', 'ctx'), may hold values from 0.05 to 0.8
Outputs:
- mixed: bfloat16 [32, 1536, 2048], P('exp', 'ctx')
The draws below stay inside these ranges and needn't reach their ends.
Inputs may be any that keep to these rules, and one draw needn't show every extreme that they name: `routes`: each row names 4 different experts; the 64 rows of one device name no expert more than 12 times, and in some devices' rows one expert exactly 12 times.
All inputs are finite; a program needn't handle non-finite values.
Results may differ from the reference program's by a relative error of at most 0.008.
Values may be sent and summed in bfloat16 or wider, within the bound.
No kernel may reach another device: no remote copies, remote signals or barrier semaphores. Data moves between devices by JAX's collectives and lax.ppermute only.
A program may use at most 64 MiB of HBM per device.

```python
import math
import jax
import jax.numpy as jnp
import numpy as np
from jax import lax

D = 2048
HEADS = 8
HEAD_DIM = 128
FFW = 512
TOP = 4
TOK_DEV = 64
SEQS = 32
LEN = 1536
EXPERTS = 32
CAP = 12
N_CTX = 24


def drawn_draw(key):
    full_shape = (SEQS, LEN, HEADS * HEAD_DIM)
    return jnp.clip(1.6 * jax.random.normal(key, full_shape, jnp.float32), -6.0, 6.0)


def draw_queries(key, part):
    drawn = drawn_draw(jax.random.fold_in(key, 1))
    return drawn.astype(jnp.bfloat16)


def draw_keys(key, part):
    drawn = drawn_draw(jax.random.fold_in(key, 2))
    return drawn.astype(jnp.bfloat16)


def level_of(own_key, shape, shards, smallest, largest):
    def one(dim, shards_of):
        heights = jax.random.uniform(jax.random.fold_in(jax.random.fold_in(own_key, 6), dim), (shards_of,), jnp.float32, smallest / len(shards), largest / len(shards))
        return jnp.repeat(jnp.exp(heights), shape[dim] // shards_of).reshape((-1,) + (1,) * (len(shape) - dim - 1))

    gain = one(*shards[0])
    for cut in shards[1:]:
        gain = gain * one(*cut)
    return gain


def assign_block(key, own, number, rows, count, top, limit, skew):
    order = jax.random.permutation(key, count)
    packed, ordinary = portions_of(count, rows * top, limit, skew, True), portions_of(count, rows * top, limit, skew, False)
    places = jnp.arange(count)

    def named(sizes, rotation):
        used = int((sizes > 0).sum())
        fixed = max(1, used // 4)
        moved = fixed + (places - fixed + rotation * (used - fixed)) % max(1, count - fixed)
        return jnp.zeros((count,), jnp.int32).at[order[jnp.where(places < fixed, places, moved)]].set(jnp.asarray(sizes, jnp.int32))

    sizes = jnp.where(number % 4 == 0, named(packed, number // 4), named(ordinary, number - number // 4 - 1))
    mixed = jax.random.permutation(jax.random.fold_in(own, 3), count)
    giver, taker = mixed[0:count // 2 * 2:2], mixed[1:count // 2 * 2:2]
    slack = jnp.minimum(sizes[giver] - 1, limit - sizes[taker]) // 2
    slack = jnp.where((giver == order[0]) | (taker == order[0]) | (sizes[taker] == 0), 0, jnp.maximum(slack, 0))
    moved = jax.random.randint(jax.random.fold_in(own, 4), (count // 2,), 0, 1 << 20) % (slack + 1)
    sizes = sizes.at[giver].add(-moved).at[taker].add(moved)
    items = jnp.searchsorted(jnp.cumsum(sizes), jnp.arange(rows * top), side="right").astype(jnp.int32)
    table = items.reshape(top, rows).T
    table = table[jax.random.permutation(jax.random.fold_in(own, 1), rows)]
    rotation = jax.random.randint(jax.random.fold_in(own, 2), (rows, 1), 0, top)
    return jnp.take_along_axis(table, (jnp.arange(top)[None, :] + rotation) % top, axis=1)


def portions_of(count, total, reach, lean, full):
    portions = [(1 << 20) // math.isqrt(standing ** lean) + 1 for standing in range(1, count + 1)]
    largest = reach if full else min(reach, max(-(-total // count), total * portions[0] // sum(portions)))
    least = 1 if total - largest >= count - 1 else 0
    counts, rest = [largest] + [least] * (count - 1), total - largest - least * (count - 1)
    while rest > 0:
        free = [i for i in range(1, count) if counts[i] < largest] or [i for i in range(1, count) if counts[i] < reach]
        mass, remaining = sum([portions[i] for i in free]), rest
        for i in free:
            more = min(reach - counts[i], max(1, remaining * portions[i] // mass), rest)
            counts[i] = counts[i] + more
            rest = rest - more
    return np.array(counts)


def scatter_about(own_key, dims, width, bound, cuts=(), held_as=jnp.bfloat16):
    values = width * jax.random.normal(own_key, dims, jnp.float32)
    if cuts:
        values = values * level_of(own_key, dims, cuts, -0.22, 0.18)
    return jnp.clip(values, -bound, bound).astype(held_as)


def setup_inputs(seed: int = 0) -> dict:
    splits = jax.random.split(jax.random.key(seed), 12)
    queries = draw_queries(jax.random.fold_in(splits[11], 71), 0)
    keys = draw_keys(jax.random.fold_in(splits[11], 71), 0)
    values = scatter_about(splits[2], (SEQS, LEN, HEADS * HEAD_DIM), 1.0, 6.0, ((0, 32), (1, 24)))
    residual = scatter_about(splits[3], (SEQS, LEN, D), 1.0, 6.0, ((0, 32), (1, 24)))
    out_proj = scatter_about(splits[4], (HEADS * HEAD_DIM, D), (HEADS * HEAD_DIM) ** -0.5, 0.1875)
    norm_gain = jnp.clip(1.0 + 0.15 * jax.random.normal(splits[5], (D,), jnp.float32), 0.25, 1.75)
    w_gate = scatter_about(splits[6], (EXPERTS, D, FFW), D ** -0.5, 0.125, ((0, 32),))
    w_up = scatter_about(splits[7], (EXPERTS, D, FFW), D ** -0.5, 0.125, ((0, 32),))
    w_down = scatter_about(splits[8], (EXPERTS, FFW, D), FFW ** -0.5, 0.25, ((0, 32),))
    routes_keys = jax.random.split(jax.random.fold_in(splits[9], 1), SEQS * LEN // TOK_DEV)
    routes_turns = jax.random.permutation(jax.random.fold_in(splits[9], 3), SEQS * LEN // TOK_DEV)
    routes = jax.vmap(lambda own, number: assign_block(jax.random.fold_in(splits[9], 2), own, number, TOK_DEV, EXPERTS, TOP, CAP, 2))(routes_keys, routes_turns).reshape((SEQS, LEN, TOP))
    route_prob = jnp.clip(jnp.exp(math.log(0.8) - 2.7725887 * jax.random.uniform(splits[10], (SEQS, LEN, TOP), jnp.float32) ** level_of(splits[10], (SEQS, LEN, TOP), ((0, 32), (1, 24)), -0.2, 0.2)), 0.05, 0.8)
    return dict(queries=queries, keys=keys, values=values, residual=residual, out_proj=out_proj, norm_gain=norm_gain, w_gate=w_gate, w_up=w_up, w_down=w_down, routes=routes, route_prob=route_prob)


def attend_sequence(inputs):
    query_seq, key_seq, value_seq = inputs
    length = query_seq.shape[0]
    query_float = query_seq.astype(jnp.float32).reshape(length, HEADS, HEAD_DIM)
    key_float = key_seq.astype(jnp.float32).reshape(length, HEADS, HEAD_DIM)
    value_float = value_seq.astype(jnp.float32).reshape(length, HEADS, HEAD_DIM)
    scores = jnp.einsum('qhd,khd->hqk', query_float, key_float) * HEAD_DIM ** (-0.5)
    positions = jnp.arange(length, dtype=jnp.int32)
    allowed = positions[None, :] <= positions[:, None]
    scores = jnp.where(allowed[None], scores, -1e+30)
    row_max = scores.max(axis=-1, keepdims=True)
    exponent = jnp.where(allowed[None], jnp.exp(scores - row_max), 0.0)
    denom = exponent.sum(axis=-1)
    rounded = lax.optimization_barrier(exponent.astype(jnp.bfloat16)).astype(jnp.float32)
    output = jnp.einsum('hqk,khd->qhd', rounded, value_float) / jnp.transpose(denom)[:, :, None]
    return output.reshape(length, HEADS * HEAD_DIM).astype(jnp.bfloat16)

def reference(queries, keys, values, residual, out_proj, norm_gain, w_gate, w_up, w_down, routes, route_prob):
    attended = lax.map(attend_sequence, (queries, keys, values))
    projected = jnp.dot(attended.reshape(-1, HEADS * HEAD_DIM), out_proj, preferred_element_type=jnp.float32)
    hidden = residual.astype(jnp.float32).reshape(-1, D) + projected
    mean_square = lax.optimization_barrier(jnp.mean(hidden * hidden, axis=-1, keepdims=True))
    normed = (hidden * lax.rsqrt(mean_square + 1e-05) * norm_gain).astype(jnp.bfloat16)
    chosen = routes.reshape(-1)
    prob_flat = route_prob.reshape(-1)
    most_rows = SEQS * N_CTX * CAP

    def per_expert(totals, expert_inputs):
        expert_id, gate_mat, up_mat, down_mat = expert_inputs
        matches = chosen == expert_id
        found = jnp.nonzero(matches, size=most_rows, fill_value=0)[0].astype(jnp.int32)
        live = jnp.arange(most_rows, dtype=jnp.int32) < jnp.sum(matches.astype(jnp.int32))
        token_rows = found // TOP
        gathered = normed[token_rows]
        gate_part = jnp.dot(gathered, gate_mat, preferred_element_type=jnp.float32)
        up_part = jnp.dot(gathered, up_mat, preferred_element_type=jnp.float32)
        activated = (jax.nn.silu(gate_part) * up_part).astype(jnp.bfloat16)
        produced = jnp.dot(activated, down_mat, preferred_element_type=jnp.float32).astype(jnp.bfloat16)
        produced = lax.optimization_barrier(produced).astype(jnp.float32)
        factor = jnp.where(live, prob_flat[found], 0.0)
        totals = totals.at[token_rows].add(factor[:, None] * produced)
        return (totals, None)
    start_totals = jnp.zeros((chosen.shape[0] // TOP, D), jnp.float32)
    expert_ids = jnp.arange(EXPERTS, dtype=jnp.int32)
    totals, unused = lax.scan(per_expert, start_totals, (expert_ids, w_gate, w_up, w_down))
    return (hidden + totals).astype(jnp.bfloat16).reshape(residual.shape)
```

```python
import jax
import jax.numpy as jnp
from jax import lax
from jax.experimental import pallas as pl
from jax.experimental.pallas import tpu as pltpu
from jax.sharding import PartitionSpec as P

HEADS = 8
HEAD_DIM = 128
TOP = 4
TOK = 64
D = 2048
FFW = 512
N_CTX = 24
EXPERTS = 32
PARTS = N_CTX // HEADS
Q_ROWS = 24
CHUNK = 2 * TOK + Q_ROWS
GROUP = 6
MAIN = 8
REST = 4
WIDE = D + D // 2
SLOT_ROWS = EXPERTS * MAIN
REST_ROWS = EXPERTS * REST
f32 = jnp.float32
bf16 = jnp.bfloat16


def dot(a, b):
    return jnp.dot(a, b, preferred_element_type=f32)


def dot_first(a, b):
    return lax.dot_general(a, b, (((0,), (0,)), ((), ())), preferred_element_type=f32)


def part_rows(part):
    return min(Q_ROWS, TOK - part * Q_ROWS)


def pack_kernel(q_ref, k_ref, v_ref, o_ref):
    for head in range(HEADS):
        cols = slice(head * HEAD_DIM, (head + 1) * HEAD_DIM)
        for part in range(PARTS):
            rows = part_rows(part)
            chunk = head * PARTS + part
            o_ref[chunk, 0:TOK, :] = k_ref[:, cols]
            o_ref[chunk, TOK : 2 * TOK, :] = v_ref[:, cols]
            o_ref[chunk, 2 * TOK : 2 * TOK + rows, :] = q_ref[
                part * Q_ROWS : part * Q_ROWS + rows, cols
            ]
            if rows < Q_ROWS:
                o_ref[chunk, 2 * TOK + rows : CHUNK, :] = jnp.zeros((Q_ROWS - rows, HEAD_DIM), bf16)


def attend_kernel(part_ref, x_ref, o_ref):
    part = part_ref[0]
    factor = HEAD_DIM ** (-0.5)
    rows = GROUP * Q_ROWS
    span = GROUP * TOK
    row = lax.broadcasted_iota(jnp.int32, (rows, span), 0)
    block = jnp.zeros((rows, span), jnp.int32)
    for b in range(1, GROUP):
        block = block + (row >= b * Q_ROWS).astype(jnp.int32)
    query_pos = row + block * (TOK - Q_ROWS) + part * Q_ROWS
    allowed = lax.broadcasted_iota(jnp.int32, (rows, span), 1) <= query_pos
    for g in range(N_CTX // GROUP):
        lo = g * GROUP
        hi = lo + GROUP
        queries = x_ref[lo:hi, 2 * TOK : CHUNK, :].reshape(rows, HEAD_DIM)
        near_keys = x_ref[lo:hi, 0:TOK, :].reshape(span, HEAD_DIM)
        near_values = x_ref[lo:hi, TOK : 2 * TOK, :].reshape(span, HEAD_DIM)
        contract = (((1,), (1,)), ((), ()))
        near = lax.dot_general(queries, near_keys, contract, preferred_element_type=f32)
        near = jnp.where(allowed, near, -1e30)
        top = jnp.max(near, axis=1, keepdims=True)
        if g:
            far_keys = x_ref[0:lo, 0:TOK, :].reshape(lo * TOK, HEAD_DIM)
            far_values = x_ref[0:lo, TOK : 2 * TOK, :].reshape(lo * TOK, HEAD_DIM)
            far = lax.dot_general(queries, far_keys, contract, preferred_element_type=f32)
            top = jnp.maximum(top, jnp.max(far, axis=1, keepdims=True))
        near_exp = jnp.where(allowed, jnp.exp((near - top) * factor), 0.0)
        total = jnp.sum(near_exp, axis=1, keepdims=True)
        acc = dot(near_exp.astype(bf16), near_values)
        if g:
            far_exp = jnp.exp((far - top) * factor)
            total = total + jnp.sum(far_exp, axis=1, keepdims=True)
            acc = acc + dot(far_exp.astype(bf16), far_values)
        o_ref[lo:hi] = (acc / total).astype(bf16).reshape(GROUP, Q_ROWS, HEAD_DIM)


def slot_values(routes):
    expert = lax.broadcasted_iota(jnp.int32, (EXPERTS, TOK), 0)
    named = jnp.zeros((EXPERTS, TOK), f32)
    for k in range(TOP):
        named = named + (routes[k : k + 1, :] == expert).astype(f32)
    earlier = (
        lax.broadcasted_iota(jnp.int32, (TOK, TOK), 0)
        < lax.broadcasted_iota(jnp.int32, (TOK, TOK), 1)
    ).astype(bf16)
    return named * (1.0 + dot(named.astype(bf16), earlier))


def spread():
    row = lax.broadcasted_iota(jnp.int32, (SLOT_ROWS, EXPERTS), 0)
    return ((row >> 3) == lax.broadcasted_iota(jnp.int32, (SLOT_ROWS, EXPERTS), 1)).astype(bf16)


def slot_masks(routes):
    value = dot(spread(), slot_values(routes).astype(bf16))
    row = lax.broadcasted_iota(jnp.int32, (SLOT_ROWS, TOK), 0)
    main = value == ((row & 7) + 1).astype(f32)
    rest = value == ((row & 3) + 1 + MAIN).astype(f32)
    low = (row & 7) < REST
    return main, rest & low, rest & (~low)


def project_kernel(a_ref, residual_ref, w_ref, gain_ref, routes_ref, hidden_ref, o_ref, rows_ref):
    for head in range(HEADS):
        cols = slice(head * HEAD_DIM, (head + 1) * HEAD_DIM)
        for part in range(PARTS):
            rows = part_rows(part)
            rows_ref[part * Q_ROWS : part * Q_ROWS + rows, cols] = a_ref[
                head * PARTS + part, 0:rows, :
            ]
    hidden = residual_ref[...].astype(f32) + dot(rows_ref[...], w_ref[...])
    hidden_ref[...] = hidden
    mean_square = jnp.mean(hidden * hidden, axis=-1, keepdims=True)
    normed = (hidden * lax.rsqrt(mean_square + 1e-05) * gain_ref[...]).astype(bf16)
    main, low, high = slot_masks(routes_ref[...])
    o_ref[:, 0:D] = dot(main.astype(bf16), normed).astype(bf16)
    o_ref[:, D:WIDE] = (
        dot(low.astype(bf16), normed[:, 0 : D // 2]) + dot(high.astype(bf16), normed[:, D // 2 : D])
    ).astype(bf16)


def picker(high):
    row = lax.broadcasted_iota(jnp.int32, (REST_ROWS, SLOT_ROWS), 0)
    col = lax.broadcasted_iota(jnp.int32, (REST_ROWS, SLOT_ROWS), 1)
    return (col == (row >> 2) * MAIN + (row & 3) + (REST if high else 0)).astype(bf16)


def expert_kernel(x_ref, gate_ref, up_ref, down_ref, o_ref, rows_ref):
    low, high = picker(False), picker(True)
    rows_ref[0:SLOT_ROWS, :] = x_ref[:, 0:D]
    rows_ref[SLOT_ROWS:, 0 : D // 2] = dot(low, x_ref[:, D:WIDE]).astype(bf16)
    rows_ref[SLOT_ROWS:, D // 2 : D] = dot(high, x_ref[:, D:WIDE]).astype(bf16)
    gate = dot(rows_ref[...], gate_ref[...])
    up = dot(rows_ref[...], up_ref[...])
    act = (gate / (1.0 + jnp.exp(-gate)) * up).astype(bf16)
    made = dot(act, down_ref[...]).astype(bf16)
    o_ref[:, 0:D] = made[0:SLOT_ROWS]
    o_ref[:, D:WIDE] = (
        dot_first(low, made[SLOT_ROWS:, 0 : D // 2]) + dot_first(high, made[SLOT_ROWS:, D // 2 : D])
    ).astype(bf16)


def mix_kernel(y_ref, hidden_ref, routes_ref, prob_ref, o_ref):
    routes = routes_ref[...]
    main, low, high = slot_masks(routes)
    expert = lax.broadcasted_iota(jnp.int32, (EXPERTS, TOK), 0)
    prob = jnp.zeros((EXPERTS, TOK), f32)
    for k in range(TOP):
        prob = prob + jnp.where(routes[k : k + 1, :] == expert, prob_ref[k : k + 1, :], 0.0)
    mixed = hidden_ref[...]
    rest = y_ref[:, D:WIDE]
    first = jnp.zeros((TOK, D // 2), f32)
    second = jnp.zeros((TOK, D // 2), f32)
    for _ in range(3):
        term = prob.astype(bf16)
        prob = prob - term.astype(f32)
        wide = dot(spread(), term)
        mixed = mixed + dot_first(jnp.where(main, wide, 0.0).astype(bf16), y_ref[:, 0:D])
        first = first + dot_first(jnp.where(low, wide, 0.0).astype(bf16), rest)
        second = second + dot_first(jnp.where(high, wide, 0.0).astype(bf16), rest)
    o_ref[:, 0 : D // 2] = (mixed[:, 0 : D // 2] + first).astype(bf16)
    o_ref[:, D // 2 : D] = (mixed[:, D // 2 : D] + second).astype(bf16)


def call(kernel, name, outs, *args, scratch=(), smem=0):
    vmem = pl.BlockSpec(memory_space=pltpu.VMEM)
    specs = [pl.BlockSpec(memory_space=pltpu.SMEM)] * smem + [vmem] * (len(args) - smem)
    many = isinstance(outs, list)
    return pl.pallas_call(
        kernel,
        out_shape=outs,
        in_specs=specs,
        out_specs=[vmem] * len(outs) if many else vmem,
        scratch_shapes=scratch,
        name=name,
        compiler_params=pltpu.CompilerParams(vmem_limit_bytes=56 * 1024 * 1024),
    )(*args)


def exchange(x, axis):
    return lax.all_to_all(x, axis, split_axis=0, concat_axis=0, tiled=True)


def local(
    queries, keys, values, residual, out_proj, norm_gain, w_gate, w_up, w_down, routes, route_prob
):
    shape = jax.ShapeDtypeStruct
    routes_t = routes[0].T
    prob_t = route_prob[0].T
    part = (lax.axis_index("ctx") % PARTS).astype(jnp.int32).reshape(1)
    packed = call(
        pack_kernel, "pack", shape((N_CTX, CHUNK, HEAD_DIM), bf16), queries[0], keys[0], values[0]
    )
    gathered = exchange(packed, "ctx")
    attended = call(
        attend_kernel, "attend", shape((N_CTX, Q_ROWS, HEAD_DIM), bf16), part, gathered, smem=1
    )
    mine = exchange(attended, "ctx")
    hidden, outgoing = call(
        project_kernel,
        "project",
        [shape((TOK, D), f32), shape((SLOT_ROWS, WIDE), bf16)],
        mine,
        residual[0],
        out_proj,
        norm_gain.reshape(1, D),
        routes_t,
        scratch=[pltpu.VMEM((TOK, HEADS * HEAD_DIM), bf16)],
    )
    incoming = exchange(outgoing.reshape(EXPERTS, MAIN, WIDE), "exp").reshape(SLOT_ROWS, WIDE)
    made = call(
        expert_kernel,
        "experts",
        shape((SLOT_ROWS, WIDE), bf16),
        incoming,
        w_gate[0],
        w_up[0],
        w_down[0],
        scratch=[pltpu.VMEM((SLOT_ROWS + REST_ROWS, D), bf16)],
    )
    returned = exchange(made.reshape(EXPERTS, MAIN, WIDE), "exp").reshape(SLOT_ROWS, WIDE)
    return call(mix_kernel, "mix", shape((TOK, D), bf16), returned, hidden, routes_t, prob_t)[None]


def solution(mesh):
    placed = (
        P("exp", "ctx", None),
        P("exp", "ctx", None),
        P("exp", "ctx", None),
        P("exp", "ctx", None),
        P(),
        P(),
        P("exp", None, None),
        P("exp", None, None),
        P("exp", None, None),
        P("exp", "ctx", None),
        P("exp", "ctx", None),
    )
    return jax.shard_map(
        local, mesh=mesh, in_specs=placed, out_specs=P("exp", "ctx", None), check_vma=False
    )
```

```python
import jax
import jax.numpy as jnp
from jax import lax
from jax.experimental import pallas as pl
from jax.experimental.pallas import tpu as pltpu
from jax.sharding import PartitionSpec as P

HEADS = 8
HEAD_DIM = 128
TOP = 4
TOK = 64
D = 2048
FFW = 512
N_CTX = 24
EXPERTS = 32
PARTS = N_CTX // HEADS
Q_ROWS = 24
CHUNK = 2 * TOK + Q_ROWS
GROUP = 6
MAIN = 8
REST = 4
HALF = D // 2
WIDE = D + HALF
SLOT_ROWS = EXPERTS * MAIN
REST_ROWS = EXPERTS * REST
f32 = jnp.float32
bf16 = jnp.bfloat16


def dot(a, b):
    return jnp.dot(a, b, preferred_element_type=f32)


def dot_first(a, b):
    return lax.dot_general(a, b, (((0,), (0,)), ((), ())), preferred_element_type=f32)


def dot_last(a, b):
    return lax.dot_general(a, b, (((1,), (1,)), ((), ())), preferred_element_type=f32)


def part_rows(part):
    return min(Q_ROWS, TOK - part * Q_ROWS)


def pack_kernel(q_ref, k_ref, v_ref, o_ref):
    for head in range(HEADS):
        cols = slice(head * HEAD_DIM, (head + 1) * HEAD_DIM)
        for part in range(PARTS):
            rows = part_rows(part)
            chunk = head * PARTS + part
            o_ref[chunk, 0:TOK, :] = k_ref[:, cols]
            o_ref[chunk, TOK : 2 * TOK, :] = v_ref[:, cols]
            o_ref[chunk, 2 * TOK : 2 * TOK + rows, :] = q_ref[
                part * Q_ROWS : part * Q_ROWS + rows, cols
            ]
            if rows < Q_ROWS:
                o_ref[chunk, 2 * TOK + rows : CHUNK, :] = jnp.zeros((Q_ROWS - rows, HEAD_DIM), bf16)


def attend_kernel(part_ref, x_ref, o_ref):
    factor = HEAD_DIM ** (-0.5) * 1.4426950408889634
    rows = GROUP * Q_ROWS
    span = GROUP * TOK
    row = lax.broadcasted_iota(jnp.int32, (rows, span), 0)
    block = jnp.zeros((rows, span), jnp.int32)
    for b in range(1, GROUP):
        block = block + (row >= b * Q_ROWS).astype(jnp.int32)
    query_pos = row + block * (TOK - Q_ROWS) + part_ref[0] * Q_ROWS
    allowed = lax.broadcasted_iota(jnp.int32, (rows, span), 1) <= query_pos
    for g in range(N_CTX // GROUP):
        lo = g * GROUP
        hi = lo + GROUP
        queries = x_ref[lo:hi, 2 * TOK : CHUNK, :].reshape(rows, HEAD_DIM)
        near_keys = x_ref[lo:hi, 0:TOK, :].reshape(span, HEAD_DIM)
        near_values = x_ref[lo:hi, TOK : 2 * TOK, :].reshape(span, HEAD_DIM)
        near = jnp.where(allowed, dot_last(queries, near_keys), -1e30)
        top = jnp.max(near, axis=1, keepdims=True)
        if g:
            far_keys = x_ref[0:lo, 0:TOK, :].reshape(lo * TOK, HEAD_DIM)
            far_values = x_ref[0:lo, TOK : 2 * TOK, :].reshape(lo * TOK, HEAD_DIM)
            far = dot_last(queries, far_keys)
            top = jnp.maximum(top, jnp.max(far, axis=1, keepdims=True))
        near_exp = jnp.exp2((near - top) * factor)
        total = jnp.sum(near_exp, axis=1, keepdims=True)
        acc = dot(near_exp.astype(bf16), near_values)
        if g:
            far_exp = jnp.exp2((far - top) * factor)
            total = total + jnp.sum(far_exp, axis=1, keepdims=True)
            acc = acc + dot(far_exp.astype(bf16), far_values)
        o_ref[lo:hi] = (acc / total).astype(bf16).reshape(GROUP, Q_ROWS, HEAD_DIM)


def plan_kernel(routes_ref, prob_ref, *outs):
    routes = routes_ref[...]
    expert = lax.broadcasted_iota(jnp.int32, (EXPERTS, TOK), 0)
    named = jnp.zeros((EXPERTS, TOK), f32)
    prob = jnp.zeros((EXPERTS, TOK), f32)
    for k in range(TOP):
        here = routes[k : k + 1, :] == expert
        named = named + here.astype(f32)
        prob = prob + jnp.where(here, prob_ref[k : k + 1, :], 0.0)
    earlier = (
        lax.broadcasted_iota(jnp.int32, (TOK, TOK), 0)
        < lax.broadcasted_iota(jnp.int32, (TOK, TOK), 1)
    ).astype(bf16)
    slot = named * (1.0 + dot(named.astype(bf16), earlier))
    spread = (
        (lax.broadcasted_iota(jnp.int32, (SLOT_ROWS, EXPERTS), 0) >> 3)
        == lax.broadcasted_iota(jnp.int32, (SLOT_ROWS, EXPERTS), 1)
    ).astype(bf16)
    value = dot(spread, slot.astype(bf16))
    row = lax.broadcasted_iota(jnp.int32, (SLOT_ROWS, TOK), 0)
    main = value == ((row & 7) + 1).astype(f32)
    rest = value == ((row & 3) + 1 + MAIN).astype(f32)
    low = (row & 7) < REST
    masks = (main, rest & low, rest & (~low))
    for mask, out in zip(masks, outs[:3]):
        out[...] = mask.astype(bf16)
    for term in range(3):
        part = prob.astype(bf16)
        prob = prob - part.astype(f32)
        wide = dot(spread, part)
        for mask, out in zip(masks, outs[3:]):
            out[term] = jnp.where(mask, wide, 0.0).astype(bf16)


def project_kernel(
    a_ref, residual_ref, w_ref, gain_ref, m_ref, l_ref, h_ref, hidden_ref, o_ref, rows_ref
):
    for head in range(HEADS):
        cols = slice(head * HEAD_DIM, (head + 1) * HEAD_DIM)
        for part in range(PARTS):
            rows = part_rows(part)
            rows_ref[part * Q_ROWS : part * Q_ROWS + rows, cols] = a_ref[
                head * PARTS + part, 0:rows, :
            ]
    hidden = residual_ref[...].astype(f32) + dot(rows_ref[...], w_ref[...])
    hidden_ref[...] = hidden
    mean_square = jnp.mean(hidden * hidden, axis=-1, keepdims=True)
    normed = (hidden * lax.rsqrt(mean_square + 1e-05) * gain_ref[...]).astype(bf16)
    o_ref[:, 0:D] = dot(m_ref[...], normed).astype(bf16)
    o_ref[:, D:WIDE] = (
        dot(l_ref[...], normed[:, 0:HALF]) + dot(h_ref[...], normed[:, HALF:D])
    ).astype(bf16)


def picker(high):
    row = lax.broadcasted_iota(jnp.int32, (REST_ROWS, SLOT_ROWS), 0)
    col = lax.broadcasted_iota(jnp.int32, (REST_ROWS, SLOT_ROWS), 1)
    return (col == (row >> 2) * MAIN + (row & 3) + (REST if high else 0)).astype(bf16)


def expert_kernel(x_ref, gate_ref, up_ref, down_ref, o_ref, rows_ref):
    low, high = picker(False), picker(True)
    rows_ref[0:SLOT_ROWS, :] = x_ref[:, 0:D]
    rows_ref[SLOT_ROWS:, 0 : HALF] = dot(low, x_ref[:, D:WIDE]).astype(bf16)
    rows_ref[SLOT_ROWS:, HALF : D] = dot(high, x_ref[:, D:WIDE]).astype(bf16)
    gate = dot(rows_ref[...], gate_ref[...])
    up = dot(rows_ref[...], up_ref[...])
    act = (gate / (1.0 + jnp.exp(-gate)) * up).astype(bf16)
    made = dot(act, down_ref[...]).astype(bf16)
    o_ref[:, 0:D] = made[0:SLOT_ROWS]
    o_ref[:, D:WIDE] = (
        dot_first(low, made[SLOT_ROWS:, 0 : HALF]) + dot_first(high, made[SLOT_ROWS:, HALF : D])
    ).astype(bf16)


def mix_kernel(y_ref, hidden_ref, m_ref, l_ref, h_ref, o_ref):
    total = hidden_ref[...]
    rest = y_ref[:, D:WIDE]
    first = jnp.zeros((TOK, HALF), f32)
    second = jnp.zeros((TOK, HALF), f32)
    for term in range(3):
        total = total + dot_first(m_ref[term], y_ref[:, 0:D])
        first = first + dot_first(l_ref[term], rest)
        second = second + dot_first(h_ref[term], rest)
    o_ref[:, 0:HALF] = (total[:, 0:HALF] + first).astype(bf16)
    o_ref[:, HALF:D] = (total[:, HALF:D] + second).astype(bf16)


def call(kernel, name, outs, *args, scratch=(), smem=0, mib=16):
    vmem = pl.BlockSpec(memory_space=pltpu.VMEM)
    specs = [pl.BlockSpec(memory_space=pltpu.SMEM)] * smem + [vmem] * (len(args) - smem)
    many = isinstance(outs, list)
    return pl.pallas_call(
        kernel,
        out_shape=outs,
        in_specs=specs,
        out_specs=[vmem] * len(outs) if many else vmem,
        scratch_shapes=scratch,
        name=name,
        compiler_params=pltpu.CompilerParams(vmem_limit_bytes=mib * 1024 * 1024),
    )(*args)


def of(*dims, dtype=bf16):
    return jax.ShapeDtypeStruct(dims, dtype)


def pack(queries, keys, values):
    return call(pack_kernel, "pack", of(N_CTX, CHUNK, HEAD_DIM), queries, keys, values, mib=8)


def attend(part, gathered):
    return call(attend_kernel, "attend", of(N_CTX, Q_ROWS, HEAD_DIM), part, gathered, smem=1)


def plan(routes, prob):
    outs = [of(SLOT_ROWS, TOK)] * 3 + [of(3, SLOT_ROWS, TOK)] * 3
    made = call(plan_kernel, "plan", outs, routes.T, prob.T, mib=8)
    return made[:3], made[3:]


def project(attended, residual, out_proj, norm_gain, masks):
    outs = [of(TOK, D, dtype=f32), of(SLOT_ROWS, WIDE)]
    scratch = [pltpu.VMEM((TOK, HEADS * HEAD_DIM), bf16)]
    gain = norm_gain.reshape(1, D)
    return call(
        project_kernel, "project", outs, attended, residual, out_proj, gain, *masks, scratch=scratch
    )


def experts(rows, w_gate, w_up, w_down):
    scratch = [pltpu.VMEM((SLOT_ROWS + REST_ROWS, D), bf16)]
    outs = of(SLOT_ROWS, WIDE)
    return call(
        expert_kernel, "experts", outs, rows, w_gate, w_up, w_down, scratch=scratch, mib=24
    )


def mix(rows, hidden, probs):
    return call(mix_kernel, "mix", of(TOK, D), rows, hidden, *probs)


def exchange(x, axis):
    return lax.all_to_all(x, axis, split_axis=0, concat_axis=0, tiled=True)


def slots_exchange(x):
    return exchange(x.reshape(EXPERTS, MAIN, WIDE), "exp").reshape(SLOT_ROWS, WIDE)


def local(
    queries, keys, values, residual, out_proj, norm_gain, w_gate, w_up, w_down, routes, route_prob
):
    part = (lax.axis_index("ctx") % PARTS).astype(jnp.int32).reshape(1)
    gathered = exchange(pack(queries[0], keys[0], values[0]), "ctx")
    masks, probs = plan(routes[0], route_prob[0])
    attended = exchange(attend(part, gathered), "ctx")
    hidden, rows = project(attended, residual[0], out_proj, norm_gain, masks)
    rows = slots_exchange(rows)
    rows = slots_exchange(experts(rows, w_gate[0], w_up[0], w_down[0]))
    return mix(rows, hidden, probs)[None]


def solution(mesh):
    placed = (
        P("exp", "ctx", None),
        P("exp", "ctx", None),
        P("exp", "ctx", None),
        P("exp", "ctx", None),
        P(),
        P(),
        P("exp", None, None),
        P("exp", None, None),
        P("exp", None, None),
        P("exp", "ctx", None),
        P("exp", "ctx", None),
    )
    return jax.shard_map(
        local, mesh=mesh, in_specs=placed, out_specs=P("exp", "ctx", None), check_vma=False
    )
```

```python
import jax
import jax.numpy as jnp
from jax import lax
from jax.experimental import pallas as pl
from jax.experimental.pallas import tpu as pltpu
from jax.sharding import Mesh
from jax.sharding import PartitionSpec as P

HEADS = 8
HEAD_DIM = 128
TOP = 4
TOK = 64
D = 2048
FFW = 512
N_CTX = 24
EXPERTS = 32
PARTS = N_CTX // HEADS
Q_ROWS = 24
CHUNK = 2 * TOK + Q_ROWS
GROUP = 6
MAIN = 8
REST = 4
HALF = D // 2
WIDE = D + HALF
MODEL = HEADS * HEAD_DIM
HALF_MODEL = MODEL // 2
WIDE_MODEL = MODEL + HALF_MODEL
SLOT_ROWS = EXPERTS * MAIN
REST_ROWS = EXPERTS * REST
LANES = 128
RING = 8
QUAD = 4
f32 = jnp.float32
bf16 = jnp.bfloat16
i32 = jnp.int32


def dot(a, b):
    return jnp.dot(a, b, preferred_element_type=f32)


def dot_first(a, b):
    return lax.dot_general(a, b, (((0,), (0,)), ((), ())), preferred_element_type=f32)


def dot_last(a, b):
    return lax.dot_general(a, b, (((1,), (1,)), ((), ())), preferred_element_type=f32)


def part_rows(part):
    return min(Q_ROWS, TOK - part * Q_ROWS)


def pack_kernel(q_ref, k_ref, v_ref, o_ref):
    for head in range(HEADS):
        cols = slice(head * HEAD_DIM, (head + 1) * HEAD_DIM)
        for part in range(PARTS):
            rows = part_rows(part)
            chunk = head * PARTS + part
            o_ref[chunk, 0:TOK, :] = k_ref[:, cols]
            o_ref[chunk, TOK : 2 * TOK, :] = v_ref[:, cols]
            o_ref[chunk, 2 * TOK : 2 * TOK + rows, :] = q_ref[
                part * Q_ROWS : part * Q_ROWS + rows, cols
            ]
            if rows < Q_ROWS:
                o_ref[chunk, 2 * TOK + rows : CHUNK, :] = jnp.zeros((Q_ROWS - rows, HEAD_DIM), bf16)


def attend_kernel(part_ref, x_ref, o_ref):
    factor = HEAD_DIM ** (-0.5) * 1.4426950408889634
    rows = GROUP * Q_ROWS
    span = GROUP * TOK
    row = lax.broadcasted_iota(jnp.int32, (rows, span), 0)
    block = jnp.zeros((rows, span), jnp.int32)
    for b in range(1, GROUP):
        block = block + (row >= b * Q_ROWS).astype(jnp.int32)
    query_pos = row + block * (TOK - Q_ROWS) + part_ref[0] * Q_ROWS
    allowed = lax.broadcasted_iota(jnp.int32, (rows, span), 1) <= query_pos
    for g in range(N_CTX // GROUP):
        lo = g * GROUP
        hi = lo + GROUP
        queries = x_ref[lo:hi, 2 * TOK : CHUNK, :].reshape(rows, HEAD_DIM)
        near_keys = x_ref[lo:hi, 0:TOK, :].reshape(span, HEAD_DIM)
        near_values = x_ref[lo:hi, TOK : 2 * TOK, :].reshape(span, HEAD_DIM)
        near = jnp.where(allowed, dot_last(queries, near_keys), -1e30)
        top = jnp.max(near, axis=1, keepdims=True)
        if g:
            far_keys = x_ref[0:lo, 0:TOK, :].reshape(lo * TOK, HEAD_DIM)
            far_values = x_ref[0:lo, TOK : 2 * TOK, :].reshape(lo * TOK, HEAD_DIM)
            far = dot_last(queries, far_keys)
            top = jnp.maximum(top, jnp.max(far, axis=1, keepdims=True))
        near_exp = jnp.exp2((near - top) * factor)
        total = jnp.sum(near_exp, axis=1, keepdims=True)
        acc = dot(near_exp.astype(bf16), near_values)
        if g:
            far_exp = jnp.exp2((far - top) * factor)
            total = total + jnp.sum(far_exp, axis=1, keepdims=True)
            acc = acc + dot(far_exp.astype(bf16), far_values)
        o_ref[lo:hi] = (acc / total).astype(bf16).reshape(GROUP, Q_ROWS, HEAD_DIM)


def slots_of(routes):
    expert = lax.broadcasted_iota(i32, (EXPERTS, TOK), 0)
    named = jnp.zeros((EXPERTS, TOK), f32)
    for k in range(TOP):
        named = named + (routes[k : k + 1, :] == expert).astype(f32)
    earlier = (
        lax.broadcasted_iota(i32, (TOK, TOK), 0) < lax.broadcasted_iota(i32, (TOK, TOK), 1)
    ).astype(bf16)
    return named * (1.0 + dot(named.astype(bf16), earlier))


def masks_of(value):
    row = lax.broadcasted_iota(i32, value.shape, 0)
    main = value == ((row & 7) + 1).astype(f32)
    rest = value == ((row & 3) + 1 + MAIN).astype(f32)
    low = (row & 7) < REST
    return main, rest & low, rest & (~low)


def stage_kernel(residual_ref, routes_ref, o_ref):
    o_ref[:, 0:D] = residual_ref[...]
    row = lax.broadcasted_iota(i32, (TOK, EXPERTS), 0)
    expert = lax.broadcasted_iota(i32, (TOK, EXPERTS), 1)
    place = ((row >> 3) == (expert >> 2)) & ((row & 7) == (expert & 3))
    values = dot(place.astype(bf16), slots_of(routes_ref[...]).astype(bf16)).astype(bf16)
    o_ref[:, D : D + LANES] = jnp.concatenate([values, jnp.zeros((TOK, LANES - TOK), bf16)], axis=1)


def select_kernel(place_ref, *refs):
    row = lax.broadcasted_iota(i32, (TOK, TOK), 0)
    col = lax.broadcasted_iota(i32, (TOK, TOK), 1)
    y = (place_ref[0] + (row >> 3)) & (RING - 1)
    line = (col == y * 8 + place_ref[1]).astype(bf16)
    for source in range(QUAD):
        rows_ref = refs[source]
        value = dot(line, rows_ref[:, D : D + LANES])[:, 0:TOK]
        main, low, high = [mask.astype(bf16) for mask in masks_of(value)]
        whole = dot(main, rows_ref[:, 0:D]).astype(bf16)
        halves = (dot(low, rows_ref[:, 0:HALF]) + dot(high, rows_ref[:, HALF:D])).astype(bf16)
        for shift in range(RING):
            part = slice(shift * MAIN, (shift + 1) * MAIN)
            refs[QUAD + shift][source, :, 0:D] = whole[part]
            refs[QUAD + shift][source, :, D:WIDE] = halves[part]


def plan_kernel(routes_ref, prob_ref, *outs):
    routes = routes_ref[...]
    expert = lax.broadcasted_iota(i32, (EXPERTS, TOK), 0)
    prob = jnp.zeros((EXPERTS, TOK), f32)
    for k in range(TOP):
        prob = prob + jnp.where(routes[k : k + 1, :] == expert, prob_ref[k : k + 1, :], 0.0)
    spread = (
        (lax.broadcasted_iota(i32, (SLOT_ROWS, EXPERTS), 0) >> 3)
        == lax.broadcasted_iota(i32, (SLOT_ROWS, EXPERTS), 1)
    ).astype(bf16)
    masks = masks_of(dot(spread, slots_of(routes).astype(bf16)))
    for mask, out in zip(masks, outs[:3]):
        out[...] = mask.astype(bf16)
    for term in range(3):
        part = prob.astype(bf16)
        prob = prob - part.astype(f32)
        wide = dot(spread, part)
        for mask, out in zip(masks, outs[3:]):
            out[term] = jnp.where(mask, wide, 0.0).astype(bf16)


def dispatch_kernel(a_ref, m_ref, l_ref, h_ref, rows_ref, o_ref):
    for head in range(HEADS):
        cols = slice(head * HEAD_DIM, (head + 1) * HEAD_DIM)
        for part in range(PARTS):
            rows = part_rows(part)
            rows_ref[part * Q_ROWS : part * Q_ROWS + rows, cols] = a_ref[
                head * PARTS + part, 0:rows, :
            ]
    o_ref[:, 0:MODEL] = dot(m_ref[...], rows_ref[...]).astype(bf16)
    o_ref[:, MODEL:WIDE_MODEL] = (
        dot(l_ref[...], rows_ref[:, 0:HALF_MODEL]) + dot(h_ref[...], rows_ref[:, HALF_MODEL:MODEL])
    ).astype(bf16)


def hidden_kernel(rows_ref, residual_ref, w_ref, o_ref):
    o_ref[...] = residual_ref[...].astype(f32) + dot(rows_ref[...], w_ref[...])


def normed_of(residual, attended, w_ref, gain_ref):
    hidden = residual.astype(f32) + dot(attended, w_ref[...])
    mean_square = jnp.mean(hidden * hidden, axis=-1, keepdims=True)
    return (hidden * lax.rsqrt(mean_square + 1e-05) * gain_ref[...]).astype(bf16)


def picker(high):
    row = lax.broadcasted_iota(jnp.int32, (REST_ROWS, SLOT_ROWS), 0)
    col = lax.broadcasted_iota(jnp.int32, (REST_ROWS, SLOT_ROWS), 1)
    return (col == (row >> 2) * MAIN + (row & 3) + (REST if high else 0)).astype(bf16)


def expert_kernel(place_ref, x_ref, gain_ref, *refs):
    slots, weights = refs[:RING], refs[RING : RING + 4]
    o_ref, main_ref, rest_ref, rows_ref, w_ref, gate_ref, up_ref, down_ref, sems = refs[RING + 4 :]
    held = (w_ref, gate_ref, up_ref, down_ref)
    copies = [
        pltpu.make_async_copy(source, target, sems.at[i])
        for i, (source, target) in enumerate(zip(weights, held))
    ]
    for copy in copies:
        copy.start()
    for shift in range(RING):
        y = (place_ref[0] - shift) & (RING - 1)
        for source in range(QUAD):
            index = y * QUAD + (place_ref[1] ^ source)
            main_ref[index] = slots[shift][source, :, 0:D]
            rest_ref[index] = slots[shift][source, :, D:WIDE]
    low, high = picker(False), picker(True)
    copies[0].wait()
    rows_ref[0:SLOT_ROWS, :] = normed_of(
        main_ref[...].reshape(SLOT_ROWS, D), x_ref[:, 0:MODEL], w_ref, gain_ref
    )
    halves = rest_ref[...].reshape(SLOT_ROWS, HALF)
    residual = jnp.concatenate([dot(low, halves), dot(high, halves)], axis=1)
    halves = x_ref[:, MODEL:WIDE_MODEL]
    attended = jnp.concatenate([dot(low, halves), dot(high, halves)], axis=1).astype(bf16)
    rows_ref[SLOT_ROWS:, :] = normed_of(residual, attended, w_ref, gain_ref)
    copies[1].wait()
    gate = dot(rows_ref[...], gate_ref[...])
    copies[2].wait()
    up = dot(rows_ref[...], up_ref[...])
    copies[3].wait()
    act = (gate / (1.0 + jnp.exp(-gate)) * up).astype(bf16)
    made = dot(act, down_ref[...]).astype(bf16)
    o_ref[:, 0:D] = made[0:SLOT_ROWS]
    o_ref[:, D:WIDE] = (
        dot_first(low, made[SLOT_ROWS:, 0:HALF]) + dot_first(high, made[SLOT_ROWS:, HALF:D])
    ).astype(bf16)


def mix_kernel(y_ref, hidden_ref, m_ref, l_ref, h_ref, o_ref):
    total = hidden_ref[...]
    rest = y_ref[:, D:WIDE]
    first = jnp.zeros((TOK, HALF), f32)
    second = jnp.zeros((TOK, HALF), f32)
    for term in range(3):
        total = total + dot_first(m_ref[term], y_ref[:, 0:D])
        first = first + dot_first(l_ref[term], rest)
        second = second + dot_first(h_ref[term], rest)
    o_ref[:, 0:HALF] = (total[:, 0:HALF] + first).astype(bf16)
    o_ref[:, HALF:D] = (total[:, HALF:D] + second).astype(bf16)


def call(kernel, outs, *args, scratch=(), smem=0, away=0, mib=16):
    vmem = pl.BlockSpec(memory_space=pltpu.VMEM)
    specs = [pl.BlockSpec(memory_space=pltpu.SMEM)] * smem + [vmem] * (len(args) - smem - away)
    many = isinstance(outs, list)
    return pl.pallas_call(
        kernel,
        out_shape=outs,
        in_specs=specs + [pl.BlockSpec(memory_space=pltpu.HBM)] * away,
        out_specs=[vmem] * len(outs) if many else vmem,
        scratch_shapes=scratch,
        compiler_params=pltpu.CompilerParams(vmem_limit_bytes=mib * 1024 * 1024),
    )(*args)


def of(*dims, dtype=bf16):
    return jax.ShapeDtypeStruct(dims, dtype)


def pack(queries, keys, values):
    return call(pack_kernel, of(N_CTX, CHUNK, HEAD_DIM), queries, keys, values, mib=56)


def attend(part, gathered):
    return call(attend_kernel, of(N_CTX, Q_ROWS, HEAD_DIM), part, gathered, smem=1)


def plan(routes, prob):
    outs = [of(SLOT_ROWS, TOK)] * 3 + [of(3, SLOT_ROWS, TOK)] * 3
    made = call(plan_kernel, outs, routes.T, prob.T, mib=8)
    return made[:3], made[3:]


def stage(residual, routes):
    return call(stage_kernel, of(TOK, D + LANES), residual, routes.T, mib=8)


def select(place, rows):
    outs = [of(QUAD, MAIN, WIDE)] * RING
    return list(call(select_kernel, outs, place, *rows, smem=1, mib=16))


def dispatch(attended, masks):
    outs = [of(TOK, MODEL), of(SLOT_ROWS, WIDE_MODEL)]
    return call(dispatch_kernel, outs, attended, *masks, mib=8)


def hidden_of(rows, residual, out_proj):
    return call(hidden_kernel, of(TOK, D, dtype=f32), rows, residual, out_proj, mib=12)


def experts(place, rows, out_proj, norm_gain, weights, slots):
    scratch = [
        pltpu.VMEM((EXPERTS, MAIN, D), bf16),
        pltpu.VMEM((EXPERTS, MAIN, HALF), bf16),
        pltpu.VMEM((SLOT_ROWS + REST_ROWS, D), bf16),
        pltpu.VMEM((MODEL, D), bf16),
        pltpu.VMEM((D, FFW), bf16),
        pltpu.VMEM((D, FFW), bf16),
        pltpu.VMEM((FFW, D), bf16),
        pltpu.SemaphoreType.DMA((4,)),
    ]
    args = (rows, norm_gain.reshape(1, D), *slots, out_proj, *weights)
    outs = of(SLOT_ROWS, WIDE)
    return call(expert_kernel, outs, place, *args, scratch=scratch, smem=1, away=4, mib=50)


def mix(rows, hidden, probs):
    return call(mix_kernel, of(TOK, D), rows, hidden, *probs)


def exchange(x, axes):
    return lax.all_to_all(x, axes, split_axis=0, concat_axis=0, tiled=True)


def slots_exchange(x):
    return exchange(x.reshape(EXPERTS, MAIN, -1), ("y", "m")).reshape(SLOT_ROWS, -1)


def layer(
    queries, keys, values, residual, out_proj, norm_gain, w_gate, w_up, w_down, routes, route_prob
):
    part = (lax.axis_index("ctx") % PARTS).astype(i32).reshape(1)
    place = jnp.stack([lax.axis_index("y"), lax.axis_index("m")]).astype(i32)
    packed = pack(queries, keys, values)
    gathered = exchange(packed, "ctx")
    rows = [stage(residual, routes)]
    for other in range(1, QUAD):
        rows.append(lax.ppermute(rows[0], "m", [(i, i ^ other) for i in range(QUAD)]))
    slots = select(place, rows)
    for shift in range(1, RING):
        pairs = [(i, (i + shift) % RING) for i in range(RING)]
        slots[shift] = lax.ppermute(slots[shift], "y", pairs)
    masks, probs = plan(routes, route_prob)
    attended = attend(part, gathered)
    attended = exchange(attended, "ctx")
    rows, x = dispatch(attended, masks)
    x = slots_exchange(x)
    hidden = hidden_of(rows, residual, out_proj)
    x = experts(place, x, out_proj, norm_gain, (w_gate, w_up, w_down), slots)
    x = slots_exchange(x)
    return mix(x, hidden, probs)


def local(*args):
    args = [a if a.ndim < 3 else a[0] for a in args]
    return layer(*args)[None]


def solution(mesh):
    cut = Mesh(mesh.devices.reshape(N_CTX, RING, QUAD), ("ctx", "y", "m"))
    exp = ("y", "m")
    placed = (
        P(exp, "ctx", None),
        P(exp, "ctx", None),
        P(exp, "ctx", None),
        P(exp, "ctx", None),
        P(),
        P(),
        P(exp, None, None),
        P(exp, None, None),
        P(exp, None, None),
        P(exp, "ctx", None),
        P(exp, "ctx", None),
    )
    return jax.shard_map(
        local, mesh=cut, in_specs=placed, out_specs=P(exp, "ctx", None), check_vma=False
    )
```

```python
import jax
import jax.numpy as jnp
from jax import lax
from jax.experimental import pallas as pl
from jax.experimental.pallas import tpu as pltpu
from jax.sharding import Mesh
from jax.sharding import PartitionSpec as P

HEADS = 8
HEAD_DIM = 128
TOP = 4
TOK = 64
D = 2048
FFW = 512
N_CTX = 24
EXPERTS = 32
PARTS = N_CTX // HEADS
Q_ROWS = 24
CHUNK = 2 * TOK + Q_ROWS
GROUP = 6
MAIN = 8
REST = 4
HALF = D // 2
WIDE = D + HALF
MODEL = HEADS * HEAD_DIM
HALF_MODEL = MODEL // 2
WIDE_MODEL = MODEL + HALF_MODEL
SLOT_ROWS = EXPERTS * MAIN
REST_ROWS = EXPERTS * REST
LANES = 128
RING = 8
QUAD = 4
FAR = 4
CODES = (0, 2, 1, 3)
f32 = jnp.float32
bf16 = jnp.bfloat16
i32 = jnp.int32


def dot(a, b):
    return jnp.dot(a, b, preferred_element_type=f32)


def dot_first(a, b):
    return lax.dot_general(a, b, (((0,), (0,)), ((), ())), preferred_element_type=f32)


def dot_last(a, b):
    return lax.dot_general(a, b, (((1,), (1,)), ((), ())), preferred_element_type=f32)


def part_rows(part):
    return min(Q_ROWS, TOK - part * Q_ROWS)


def pack_kernel(q_ref, k_ref, v_ref, o_ref):
    for head in range(HEADS):
        cols = slice(head * HEAD_DIM, (head + 1) * HEAD_DIM)
        for part in range(PARTS):
            rows = part_rows(part)
            chunk = head * PARTS + part
            o_ref[chunk, 0:TOK, :] = k_ref[:, cols]
            o_ref[chunk, TOK : 2 * TOK, :] = v_ref[:, cols]
            o_ref[chunk, 2 * TOK : 2 * TOK + rows, :] = q_ref[
                part * Q_ROWS : part * Q_ROWS + rows, cols
            ]
            if rows < Q_ROWS:
                o_ref[chunk, 2 * TOK + rows : CHUNK, :] = jnp.zeros((Q_ROWS - rows, HEAD_DIM), bf16)


def attend_kernel(part_ref, x_ref, o_ref):
    factor = HEAD_DIM ** (-0.5) * 1.4426950408889634
    rows = GROUP * Q_ROWS
    span = GROUP * TOK
    row = lax.broadcasted_iota(jnp.int32, (rows, span), 0)
    block = jnp.zeros((rows, span), jnp.int32)
    for b in range(1, GROUP):
        block = block + (row >= b * Q_ROWS).astype(jnp.int32)
    query_pos = row + block * (TOK - Q_ROWS) + part_ref[0] * Q_ROWS
    allowed = lax.broadcasted_iota(jnp.int32, (rows, span), 1) <= query_pos
    for g in range(N_CTX // GROUP):
        lo = g * GROUP
        hi = lo + GROUP
        queries = x_ref[lo:hi, 2 * TOK : CHUNK, :].reshape(rows, HEAD_DIM)
        near_keys = x_ref[lo:hi, 0:TOK, :].reshape(span, HEAD_DIM)
        near_values = x_ref[lo:hi, TOK : 2 * TOK, :].reshape(span, HEAD_DIM)
        near = jnp.where(allowed, dot_last(queries, near_keys), -1e30)
        top = jnp.max(near, axis=1, keepdims=True)
        if g:
            far_keys = x_ref[0:lo, 0:TOK, :].reshape(lo * TOK, HEAD_DIM)
            far_values = x_ref[0:lo, TOK : 2 * TOK, :].reshape(lo * TOK, HEAD_DIM)
            far = dot_last(queries, far_keys)
            top = jnp.maximum(top, jnp.max(far, axis=1, keepdims=True))
        near_exp = jnp.exp2((near - top) * factor)
        total = jnp.sum(near_exp, axis=1, keepdims=True)
        acc = dot(near_exp.astype(bf16), near_values)
        if g:
            far_exp = jnp.exp2((far - top) * factor)
            total = total + jnp.sum(far_exp, axis=1, keepdims=True)
            acc = acc + dot(far_exp.astype(bf16), far_values)
        o_ref[lo:hi] = (acc / total).astype(bf16).reshape(GROUP, Q_ROWS, HEAD_DIM)


def slots_of(routes):
    expert = lax.broadcasted_iota(i32, (EXPERTS, TOK), 0)
    named = jnp.zeros((EXPERTS, TOK), f32)
    for k in range(TOP):
        named = named + (routes[k : k + 1, :] == expert).astype(f32)
    earlier = (
        lax.broadcasted_iota(i32, (TOK, TOK), 0) < lax.broadcasted_iota(i32, (TOK, TOK), 1)
    ).astype(bf16)
    return named * (1.0 + dot(named.astype(bf16), earlier))


def masks_of(value):
    row = lax.broadcasted_iota(i32, value.shape, 0)
    main = value == ((row & 7) + 1).astype(f32)
    rest = value == ((row & 3) + 1 + MAIN).astype(f32)
    low = (row & 7) < REST
    return main, rest & low, rest & (~low)


def stage_kernel(residual_ref, routes_ref, o_ref):
    o_ref[:, 0:D] = residual_ref[...]
    row = lax.broadcasted_iota(i32, (TOK, EXPERTS), 0)
    expert = lax.broadcasted_iota(i32, (TOK, EXPERTS), 1)
    place = ((row >> 3) == (expert >> 2)) & ((row & 7) == (expert & 3))
    values = dot(place.astype(bf16), slots_of(routes_ref[...]).astype(bf16)).astype(bf16)
    o_ref[:, D : D + LANES] = jnp.concatenate([values, jnp.zeros((TOK, LANES - TOK), bf16)], axis=1)


def select_kernel(place_ref, *refs):
    m = place_ref[1]
    step = 2 * (m & 1) - 1
    row = lax.broadcasted_iota(i32, (TOK, TOK), 0) >> 3
    col = lax.broadcasted_iota(i32, (TOK, TOK), 1)
    other = row > FAR
    y = (place_ref[0] + step * jnp.where(other, row - FAR, row)) & (RING - 1)
    line = (col == y * 8 + jnp.where(other, m ^ 1, m)).astype(bf16)
    own_ref, far_ref, *pair_refs = refs[3:]
    mine_ref, beside_ref, others_ref = refs[:3]
    for source, rows_ref in enumerate((mine_ref, beside_ref, others_ref.at[0], others_ref.at[1])):
        value = dot(line, rows_ref[:, D : D + LANES])[:, 0:TOK]
        main, low, high = [mask.astype(bf16) for mask in masks_of(value)]
        whole = dot(main, rows_ref[:, 0:D]).astype(bf16)
        halves = (dot(low, rows_ref[:, 0:HALF]) + dot(high, rows_ref[:, HALF:D])).astype(bf16)
        for index in range(2 * FAR):
            part = slice(index * MAIN, (index + 1) * MAIN)
            if index == 0:
                out = own_ref.at[source]
            elif index == FAR:
                out = far_ref.at[source]
            else:
                out = pair_refs[index % FAR - 1].at[index // FAR, source]
            out[:, 0:D] = whole[part]
            out[:, D:WIDE] = halves[part]


def order_kernel(place_ref, own_ref, far_ref, *refs):
    pair_refs, (mate_ref, o_ref, main_ref, rest_ref) = refs[: FAR - 1], refs[FAR - 1 :]
    y, m = place_ref[0], place_ref[1]
    step = 2 * (m & 1) - 1

    def put(ref, index, away, flip):
        row = (y + away) & (RING - 1)
        for source in range(QUAD):
            target = row * QUAD + (m ^ flip ^ CODES[source])
            main_ref[target] = ref[(*index, source)][:, 0:D]
            rest_ref[target] = ref[(*index, source)][:, D:WIDE]

    put(own_ref, (), 0, 0)
    put(far_ref, (), FAR, 0)
    for j in range(1, FAR):
        put(pair_refs[j - 1], (0,), -step * j, 0)
        put(mate_ref, (j - 1,), step * j, 1)
    o_ref[0:SLOT_ROWS, :] = main_ref[...].reshape(SLOT_ROWS, D)
    halves = rest_ref[...].reshape(SLOT_ROWS, HALF)
    o_ref[SLOT_ROWS:, 0:HALF] = dot(picker(False), halves).astype(bf16)
    o_ref[SLOT_ROWS:, HALF:D] = dot(picker(True), halves).astype(bf16)


def plan_kernel(routes_ref, prob_ref, *outs):
    routes = routes_ref[...]
    expert = lax.broadcasted_iota(i32, (EXPERTS, TOK), 0)
    prob = jnp.zeros((EXPERTS, TOK), f32)
    for k in range(TOP):
        prob = prob + jnp.where(routes[k : k + 1, :] == expert, prob_ref[k : k + 1, :], 0.0)
    spread = (
        (lax.broadcasted_iota(i32, (SLOT_ROWS, EXPERTS), 0) >> 3)
        == lax.broadcasted_iota(i32, (SLOT_ROWS, EXPERTS), 1)
    ).astype(bf16)
    masks = masks_of(dot(spread, slots_of(routes).astype(bf16)))
    for mask, out in zip(masks, outs[:3]):
        out[...] = mask.astype(bf16)
    for term in range(3):
        part = prob.astype(bf16)
        prob = prob - part.astype(f32)
        wide = dot(spread, part)
        for mask, out in zip(masks, outs[3:]):
            out[term] = jnp.where(mask, wide, 0.0).astype(bf16)


def dispatch_kernel(a_ref, m_ref, l_ref, h_ref, rows_ref, o_ref):
    for head in range(HEADS):
        cols = slice(head * HEAD_DIM, (head + 1) * HEAD_DIM)
        for part in range(PARTS):
            rows = part_rows(part)
            rows_ref[part * Q_ROWS : part * Q_ROWS + rows, cols] = a_ref[
                head * PARTS + part, 0:rows, :
            ]
    o_ref[:, 0:MODEL] = dot(m_ref[...], rows_ref[...]).astype(bf16)
    o_ref[:, MODEL:WIDE_MODEL] = (
        dot(l_ref[...], rows_ref[:, 0:HALF_MODEL]) + dot(h_ref[...], rows_ref[:, HALF_MODEL:MODEL])
    ).astype(bf16)


def hidden_kernel(rows_ref, residual_ref, w_ref, o_ref):
    o_ref[...] = residual_ref[...].astype(f32) + dot(rows_ref[...], w_ref[...])


def normed_of(residual, attended, w_ref, gain_ref):
    hidden = residual.astype(f32) + dot(attended, w_ref[...])
    mean_square = jnp.mean(hidden * hidden, axis=-1, keepdims=True)
    return (hidden * lax.rsqrt(mean_square + 1e-05) * gain_ref[...]).astype(bf16)


def picker(high):
    row = lax.broadcasted_iota(jnp.int32, (REST_ROWS, SLOT_ROWS), 0)
    col = lax.broadcasted_iota(jnp.int32, (REST_ROWS, SLOT_ROWS), 1)
    return (col == (row >> 2) * MAIN + (row & 3) + (REST if high else 0)).astype(bf16)


def expert_kernel(x_ref, residual_ref, w_ref, gain_ref, *refs):
    weights, (o_ref, rows_ref, *held, sems) = refs[:3], refs[3:]
    gate_ref, up_ref, down_ref = held
    copies = [
        pltpu.make_async_copy(source, target, sems.at[i])
        for i, (source, target) in enumerate(zip(weights, held))
    ]
    for copy in copies:
        copy.start()
    low, high = picker(False), picker(True)
    main = slice(0, SLOT_ROWS)
    rest = slice(SLOT_ROWS, SLOT_ROWS + REST_ROWS)
    rows_ref[main, :] = normed_of(residual_ref[main, :], x_ref[:, 0:MODEL], w_ref, gain_ref)
    halves = x_ref[:, MODEL:WIDE_MODEL]
    attended = jnp.concatenate([dot(low, halves), dot(high, halves)], axis=1).astype(bf16)
    rows_ref[rest, :] = normed_of(residual_ref[rest, :], attended, w_ref, gain_ref)
    copies[0].wait()
    gate = dot(rows_ref[...], gate_ref[...])
    copies[1].wait()
    up = dot(rows_ref[...], up_ref[...])
    act = (gate / (1.0 + jnp.exp(-gate)) * up).astype(bf16)
    copies[2].wait()
    made = dot(act, down_ref[...]).astype(bf16)
    o_ref[:, 0:D] = made[main]
    o_ref[:, D:WIDE] = (
        dot_first(low, made[rest, 0:HALF]) + dot_first(high, made[rest, HALF:D])
    ).astype(bf16)


def mix_kernel(y_ref, hidden_ref, m_ref, l_ref, h_ref, o_ref):
    total = hidden_ref[...]
    rest = y_ref[:, D:WIDE]
    first = jnp.zeros((TOK, HALF), f32)
    second = jnp.zeros((TOK, HALF), f32)
    for term in range(3):
        total = total + dot_first(m_ref[term], y_ref[:, 0:D])
        first = first + dot_first(l_ref[term], rest)
        second = second + dot_first(h_ref[term], rest)
    o_ref[:, 0:HALF] = (total[:, 0:HALF] + first).astype(bf16)
    o_ref[:, HALF:D] = (total[:, HALF:D] + second).astype(bf16)


def call(kernel, outs, *args, scratch=(), smem=0, away=0, mib=16):
    vmem = pl.BlockSpec(memory_space=pltpu.VMEM)
    specs = [pl.BlockSpec(memory_space=pltpu.SMEM)] * smem + [vmem] * (len(args) - smem - away)
    many = isinstance(outs, list)
    return pl.pallas_call(
        kernel,
        out_shape=outs,
        in_specs=specs + [pl.BlockSpec(memory_space=pltpu.HBM)] * away,
        out_specs=[vmem] * len(outs) if many else vmem,
        scratch_shapes=scratch,
        compiler_params=pltpu.CompilerParams(vmem_limit_bytes=mib * 1024 * 1024),
    )(*args)


def of(*dims, dtype=bf16):
    return jax.ShapeDtypeStruct(dims, dtype)


def pack(queries, keys, values):
    return call(pack_kernel, of(N_CTX, CHUNK, HEAD_DIM), queries, keys, values, mib=56)


def attend(part, gathered):
    return call(attend_kernel, of(N_CTX, Q_ROWS, HEAD_DIM), part, gathered, smem=1)


def plan(routes, prob):
    outs = [of(SLOT_ROWS, TOK)] * 3 + [of(3, SLOT_ROWS, TOK)] * 3
    made = call(plan_kernel, outs, routes.T, prob.T, mib=8)
    return made[:3], made[3:]


def stage(residual, routes):
    return call(stage_kernel, of(TOK, D + LANES), residual, routes.T, mib=8)


def select(place, rows):
    outs = [of(QUAD, MAIN, WIDE)] * 2 + [of(2, QUAD, MAIN, WIDE)] * (FAR - 1)
    own, far, *pairs = call(select_kernel, outs, place, *rows, smem=1, mib=16)
    return own, far, pairs


def order(place, own, far, pairs, mate):
    scratch = [pltpu.VMEM((EXPERTS, MAIN, D), bf16), pltpu.VMEM((EXPERTS, MAIN, HALF), bf16)]
    args = (place, own, far, *pairs, mate)
    outs = of(SLOT_ROWS + REST_ROWS, D)
    return call(order_kernel, outs, *args, scratch=scratch, smem=1, mib=12)


def dispatch(attended, masks):
    outs = [of(TOK, MODEL), of(SLOT_ROWS, WIDE_MODEL)]
    return call(dispatch_kernel, outs, attended, *masks, mib=8)


def hidden_of(rows, residual, out_proj):
    return call(hidden_kernel, of(TOK, D, dtype=f32), rows, residual, out_proj, mib=12)


def experts(rows, residual, out_proj, norm_gain, weights):
    scratch = [
        pltpu.VMEM((SLOT_ROWS + REST_ROWS, D), bf16),
        pltpu.VMEM((D, FFW), bf16),
        pltpu.VMEM((D, FFW), bf16),
        pltpu.VMEM((FFW, D), bf16),
        pltpu.SemaphoreType.DMA((3,)),
    ]
    args = (rows, residual, out_proj, norm_gain.reshape(1, D), *weights)
    outs = of(SLOT_ROWS, WIDE)
    return call(expert_kernel, outs, *args, scratch=scratch, away=3, mib=51)


def mix(rows, hidden, probs):
    return call(mix_kernel, of(TOK, D), rows, hidden, *probs)


def exchange(x, axes):
    return lax.all_to_all(x, axes, split_axis=0, concat_axis=0, tiled=True)


def slots_exchange(x):
    return exchange(x.reshape(EXPERTS, MAIN, -1), ("y", "m")).reshape(SLOT_ROWS, -1)


def shift_pairs(j):
    pairs = []
    for y in range(RING):
        for m in range(QUAD):
            to = (y + (j if m & 1 else -j)) % RING
            pairs.append((y * QUAD + m, to * QUAD + m))
    return pairs


def layer(
    queries, keys, values, residual, out_proj, norm_gain, w_gate, w_up, w_down, routes, route_prob
):
    part = (lax.axis_index("ctx") % PARTS).astype(i32).reshape(1)
    place = jnp.stack([lax.axis_index("y"), lax.axis_index("m")]).astype(i32)
    packed = pack(queries, keys, values)
    gathered = exchange(packed, "ctx")
    mine = stage(residual, routes)
    beside = lax.ppermute(mine, "m", [(i, i ^ 2) for i in range(QUAD)])
    both = jnp.stack([mine, beside])
    others = lax.ppermute(both, "m", [(i, i ^ 1) for i in range(QUAD)])
    own, far, pairs = select(place, (mine, beside, others))
    far = lax.ppermute(far, "y", [(i, (i + FAR) % RING) for i in range(RING)])
    for j in range(1, FAR):
        pairs[j - 1] = lax.ppermute(pairs[j - 1], ("y", "m"), shift_pairs(j))
    masks, probs = plan(routes, route_prob)
    attended = attend(part, gathered)
    attended = exchange(attended, "ctx")
    rows, x = dispatch(attended, masks)
    x = slots_exchange(x)
    hidden = hidden_of(rows, residual, out_proj)
    mate = jnp.stack([pair[1] for pair in pairs])
    mate = lax.ppermute(mate, "m", [(i, i ^ 1) for i in range(QUAD)])
    ordered = order(place, own, far, pairs, mate)
    x = experts(x, ordered, out_proj, norm_gain, (w_gate, w_up, w_down))
    x = slots_exchange(x)
    return mix(x, hidden, probs)


def local(*args):
    args = [a if a.ndim < 3 else a[0] for a in args]
    return layer(*args)[None]


def solution(mesh):
    cut = Mesh(mesh.devices.reshape(N_CTX, RING, QUAD), ("ctx", "y", "m"))
    exp = ("y", "m")
    placed = (
        P(exp, "ctx", None),
        P(exp, "ctx", None),
        P(exp, "ctx", None),
        P(exp, "ctx", None),
        P(),
        P(),
        P(exp, None, None),
        P(exp, None, None),
        P(exp, None, None),
        P(exp, "ctx", None),
        P(exp, "ctx", None),
    )
    return jax.shard_map(
        local, mesh=cut, in_specs=placed, out_specs=P(exp, "ctx", None), check_vma=False
    )
```

```python
import jax
import jax.numpy as jnp
from jax import lax
from jax.experimental import pallas as pl
from jax.experimental.pallas import tpu as pltpu
from jax.sharding import Mesh
from jax.sharding import PartitionSpec as P

HEADS = 8
HEAD_DIM = 128
TOP = 4
TOK = 64
D = 2048
N_CTX = 24
EXPERTS = 32
PARTS = N_CTX // HEADS
Q_ROWS = 24
CHUNK = 2 * TOK + Q_ROWS
GROUP = 8
MAIN = 8
REST = 4
HALF = D // 2
WIDE = D + HALF
MODEL = HEADS * HEAD_DIM
HALF_MODEL = MODEL // 2
WIDE_MODEL = MODEL + HALF_MODEL
SLOT_ROWS = EXPERTS * MAIN
REST_ROWS = EXPERTS * REST
LANES = 128
RING = 8
QUAD = 4
FAR = 4
CODES = (0, 2, 1, 3)
f32 = jnp.float32
bf16 = jnp.bfloat16
i32 = jnp.int32


def dot(a, b):
    return jnp.dot(a, b, preferred_element_type=f32)


def dot_first(a, b):
    return lax.dot_general(a, b, (((0,), (0,)), ((), ())), preferred_element_type=f32)


def dot_last(a, b):
    return lax.dot_general(a, b, (((1,), (1,)), ((), ())), preferred_element_type=f32)


def part_rows(part):
    return min(Q_ROWS, TOK - part * Q_ROWS)


def pack_kernel(q_ref, k_ref, v_ref, o_ref):
    for head in range(HEADS):
        cols = slice(head * HEAD_DIM, (head + 1) * HEAD_DIM)
        for part in range(PARTS):
            rows = part_rows(part)
            chunk = head * PARTS + part
            o_ref[chunk, 0:TOK, :] = k_ref[:, cols]
            o_ref[chunk, TOK : 2 * TOK, :] = v_ref[:, cols]
            o_ref[chunk, 2 * TOK : 2 * TOK + rows, :] = q_ref[
                part * Q_ROWS : part * Q_ROWS + rows, cols
            ]
            if rows < Q_ROWS:
                o_ref[chunk, 2 * TOK + rows : CHUNK, :] = jnp.zeros((Q_ROWS - rows, HEAD_DIM), bf16)


def attend_kernel(part_ref, x_ref, o_ref):
    factor = HEAD_DIM ** (-0.5) * 1.4426950408889634
    rows = GROUP * Q_ROWS
    span = GROUP * TOK
    row = lax.broadcasted_iota(jnp.int32, (rows, span), 0)
    block = jnp.zeros((rows, span), jnp.int32)
    for b in range(1, GROUP):
        block = block + (row >= b * Q_ROWS).astype(jnp.int32)
    query_pos = row + block * (TOK - Q_ROWS) + part_ref[0] * Q_ROWS
    allowed = lax.broadcasted_iota(jnp.int32, (rows, span), 1) <= query_pos
    for g in range(N_CTX // GROUP):
        lo = g * GROUP
        hi = lo + GROUP
        queries = x_ref[lo:hi, 2 * TOK : CHUNK, :].reshape(rows, HEAD_DIM)
        near_keys = x_ref[lo:hi, 0:TOK, :].reshape(span, HEAD_DIM)
        near_values = x_ref[lo:hi, TOK : 2 * TOK, :].reshape(span, HEAD_DIM)
        near = jnp.where(allowed, dot_last(queries, near_keys), -1e30)
        top = jnp.max(near, axis=1, keepdims=True)
        if g:
            far_keys = x_ref[0:lo, 0:TOK, :].reshape(lo * TOK, HEAD_DIM)
            far_values = x_ref[0:lo, TOK : 2 * TOK, :].reshape(lo * TOK, HEAD_DIM)
            far = dot_last(queries, far_keys)
            top = jnp.maximum(top, jnp.max(far, axis=1, keepdims=True))
        near_exp = jnp.exp2((near - top) * factor)
        total = jnp.sum(near_exp, axis=1, keepdims=True)
        acc = dot(near_exp.astype(bf16), near_values)
        if g:
            far_exp = jnp.exp2((far - top) * factor)
            total = total + jnp.sum(far_exp, axis=1, keepdims=True)
            acc = acc + dot(far_exp.astype(bf16), far_values)
        o_ref[lo:hi] = (acc / total).astype(bf16).reshape(GROUP, Q_ROWS, HEAD_DIM)


def slots_of(routes):
    expert = lax.broadcasted_iota(i32, (EXPERTS, TOK), 0)
    named = jnp.zeros((EXPERTS, TOK), f32)
    for k in range(TOP):
        named = named + (routes[k : k + 1, :] == expert).astype(f32)
    earlier = (
        lax.broadcasted_iota(i32, (TOK, TOK), 0) < lax.broadcasted_iota(i32, (TOK, TOK), 1)
    ).astype(bf16)
    return named * (1.0 + dot(named.astype(bf16), earlier))


def masks_of(value):
    row = lax.broadcasted_iota(i32, value.shape, 0)
    main = value == ((row & 7) + 1).astype(f32)
    rest = value == ((row & 3) + 1 + MAIN).astype(f32)
    low = (row & 7) < REST
    return main, rest & low, rest & (~low)


def stage_kernel(residual_ref, routes_ref, o_ref):
    o_ref[:, 0:D] = residual_ref[...]
    row = lax.broadcasted_iota(i32, (TOK, EXPERTS), 0)
    expert = lax.broadcasted_iota(i32, (TOK, EXPERTS), 1)
    place = ((row >> 3) == (expert >> 2)) & ((row & 7) == (expert & 3))
    values = dot(place.astype(bf16), slots_of(routes_ref[...]).astype(bf16)).astype(bf16)
    o_ref[:, D : D + LANES] = jnp.concatenate([values, jnp.zeros((TOK, LANES - TOK), bf16)], axis=1)


def select_kernel(place_ref, *refs):
    m = place_ref[1]
    step = 2 * (m & 1) - 1
    row = lax.broadcasted_iota(i32, (TOK, TOK), 0) >> 3
    col = lax.broadcasted_iota(i32, (TOK, TOK), 1)
    other = row > FAR
    y = (place_ref[0] + step * jnp.where(other, row - FAR, row)) & (RING - 1)
    line = (col == y * 8 + jnp.where(other, m ^ 1, m)).astype(bf16)
    own_ref, far_ref, *pair_refs = refs[3:]
    mine_ref, beside_ref, others_ref = refs[:3]
    for source, rows_ref in enumerate((mine_ref, beside_ref, others_ref.at[0], others_ref.at[1])):
        value = dot(line, rows_ref[:, D : D + LANES])[:, 0:TOK]
        main, low, high = [mask.astype(bf16) for mask in masks_of(value)]
        whole = dot(main, rows_ref[:, 0:D]).astype(bf16)
        halves = (dot(low, rows_ref[:, 0:HALF]) + dot(high, rows_ref[:, HALF:D])).astype(bf16)
        for index in range(2 * FAR):
            part = slice(index * MAIN, (index + 1) * MAIN)
            if index == 0:
                out = own_ref.at[source]
            elif index == FAR:
                out = far_ref.at[source]
            else:
                out = pair_refs[index % FAR - 1].at[index // FAR, source]
            out[:, 0:D] = whole[part]
            out[:, D:WIDE] = halves[part]


def order_kernel(place_ref, own_ref, far_ref, *refs):
    pair_refs, (mate_ref, o_ref, main_ref, rest_ref) = refs[: FAR - 1], refs[FAR - 1 :]
    y, m = place_ref[0], place_ref[1]
    step = 2 * (m & 1) - 1

    def put(ref, index, away, flip):
        row = (y + away) & (RING - 1)
        for source in range(QUAD):
            target = row * QUAD + (m ^ flip ^ CODES[source])
            main_ref[target] = ref[(*index, source)][:, 0:D]
            rest_ref[target] = ref[(*index, source)][:, D:WIDE]

    put(own_ref, (), 0, 0)
    put(far_ref, (), FAR, 0)
    for j in range(1, FAR):
        put(pair_refs[j - 1], (0,), -step * j, 0)
        put(mate_ref, (j - 1,), step * j, 1)
    o_ref[0:SLOT_ROWS, :] = main_ref[...].reshape(SLOT_ROWS, D)
    halves = rest_ref[...].reshape(SLOT_ROWS, HALF)
    o_ref[SLOT_ROWS:, 0:HALF] = dot(picker(False), halves).astype(bf16)
    o_ref[SLOT_ROWS:, HALF:D] = dot(picker(True), halves).astype(bf16)


def plan_kernel(routes_ref, prob_ref, *outs):
    routes = routes_ref[...]
    expert = lax.broadcasted_iota(i32, (EXPERTS, TOK), 0)
    prob = jnp.zeros((EXPERTS, TOK), f32)
    for k in range(TOP):
        prob = prob + jnp.where(routes[k : k + 1, :] == expert, prob_ref[k : k + 1, :], 0.0)
    spread = (
        (lax.broadcasted_iota(i32, (SLOT_ROWS, EXPERTS), 0) >> 3)
        == lax.broadcasted_iota(i32, (SLOT_ROWS, EXPERTS), 1)
    ).astype(bf16)
    masks = masks_of(dot(spread, slots_of(routes).astype(bf16)))
    for mask, out in zip(masks, outs[:3]):
        out[...] = mask.astype(bf16)
    terms = []
    for _ in range(3):
        terms.append(prob.astype(bf16))
        prob = prob - terms[-1].astype(f32)
    wide = [dot(spread, term) for term in terms]
    for mask, out in zip(masks, outs[3:]):
        out[...] = jnp.concatenate([jnp.where(mask, w, 0.0) for w in wide], axis=1).astype(bf16)


def dispatch_kernel(a_ref, m_ref, l_ref, h_ref, rows_ref, o_ref):
    for head in range(HEADS):
        cols = slice(head * HEAD_DIM, (head + 1) * HEAD_DIM)
        for part in range(PARTS):
            rows = part_rows(part)
            rows_ref[part * Q_ROWS : part * Q_ROWS + rows, cols] = a_ref[
                head * PARTS + part, 0:rows, :
            ]
    o_ref[:, 0:MODEL] = dot(m_ref[...], rows_ref[...]).astype(bf16)
    o_ref[:, MODEL:WIDE_MODEL] = (
        dot(l_ref[...], rows_ref[:, 0:HALF_MODEL]) + dot(h_ref[...], rows_ref[:, HALF_MODEL:MODEL])
    ).astype(bf16)


def hidden_kernel(rows_ref, residual_ref, w_ref, o_ref):
    o_ref[...] = residual_ref[...].astype(f32) + dot(rows_ref[...], w_ref[...])


def picker(high):
    row = lax.broadcasted_iota(jnp.int32, (REST_ROWS, SLOT_ROWS), 0)
    col = lax.broadcasted_iota(jnp.int32, (REST_ROWS, SLOT_ROWS), 1)
    return (col == (row >> 2) * MAIN + (row & 3) + (REST if high else 0)).astype(bf16)


def expert_kernel(x_ref, residual_ref, gain_ref, *refs):
    weights, (o_ref, rows_ref, hidden_ref, w_ref, gate_ref, up_ref, down_ref, sems) = refs[:4], refs[4:]
    halves = (slice(0, HALF), slice(HALF, D))
    pairs = [(weights[0].at[:, cols], w_ref.at[:, cols]) for cols in halves]
    pairs += list(zip(weights[1:], (gate_ref, up_ref, down_ref)))
    copies = [
        pltpu.make_async_copy(source, target, sems.at[i])
        for i, (source, target) in enumerate(pairs)
    ]
    for copy in copies:
        copy.start()
    low, high = picker(False), picker(True)
    main = slice(0, SLOT_ROWS)
    rest = slice(SLOT_ROWS, SLOT_ROWS + REST_ROWS)
    tail = x_ref[:, MODEL:WIDE_MODEL]
    tail = jnp.concatenate([dot(low, tail), dot(high, tail)], axis=1).astype(bf16)
    attended = ((main, x_ref[:, 0:MODEL]), (rest, tail))
    squares = [0.0, 0.0]
    for copy, cols in zip(copies, halves):
        copy.wait()
        for i, (rows, have) in enumerate(attended):
            hidden = residual_ref[rows, cols].astype(f32) + dot(have, w_ref[:, cols])
            squares[i] += jnp.sum(hidden * hidden, axis=-1, keepdims=True)
            hidden_ref[rows, cols] = hidden
    for (rows, _), square in zip(attended, squares):
        factor = lax.rsqrt(square * (1.0 / D) + 1e-05)
        rows_ref[rows, :] = (hidden_ref[rows, :] * factor * gain_ref[...]).astype(bf16)
    copies[2].wait()
    gate = dot(rows_ref[...], gate_ref[...])
    copies[3].wait()
    up = dot(rows_ref[...], up_ref[...])
    act = (gate / (1.0 + jnp.exp(-gate)) * up).astype(bf16)
    copies[4].wait()
    made = dot(act, down_ref[...]).astype(bf16)
    o_ref[:, 0:D] = made[main]
    o_ref[:, D:WIDE] = (
        dot_first(low, made[rest, 0:HALF]) + dot_first(high, made[rest, HALF:D])
    ).astype(bf16)


def mix_kernel(y_ref, hidden_ref, m_ref, l_ref, h_ref, o_ref):
    def terms(p_ref, rows):
        made = dot_first(p_ref[...], rows)
        return made[0:TOK] + made[TOK : 2 * TOK] + made[2 * TOK :]

    total = hidden_ref[...] + terms(m_ref, y_ref[:, 0:D])
    rest = y_ref[:, D:WIDE]
    o_ref[:, 0:HALF] = (total[:, 0:HALF] + terms(l_ref, rest)).astype(bf16)
    o_ref[:, HALF:D] = (total[:, HALF:D] + terms(h_ref, rest)).astype(bf16)


def call(kernel, outs, *args, scratch=(), smem=0, away=0, mib=16):
    vmem = pl.BlockSpec(memory_space=pltpu.VMEM)
    specs = [pl.BlockSpec(memory_space=pltpu.SMEM)] * smem + [vmem] * (len(args) - smem - away)
    many = isinstance(outs, list)
    return pl.pallas_call(
        kernel,
        out_shape=outs,
        in_specs=specs + [pl.BlockSpec(memory_space=pltpu.HBM)] * away,
        out_specs=[vmem] * len(outs) if many else vmem,
        scratch_shapes=scratch,
        compiler_params=pltpu.CompilerParams(vmem_limit_bytes=mib * 1024 * 1024),
    )(*args)


def of(*dims, dtype=bf16):
    return jax.ShapeDtypeStruct(dims, dtype)


def pack(queries, keys, values):
    return call(pack_kernel, of(N_CTX, CHUNK, HEAD_DIM), queries, keys, values, mib=56)


def attend(part, gathered):
    return call(attend_kernel, of(N_CTX, Q_ROWS, HEAD_DIM), part, gathered, smem=1)


def plan(routes, prob):
    outs = [of(SLOT_ROWS, TOK)] * 3 + [of(SLOT_ROWS, 3 * TOK)] * 3
    made = call(plan_kernel, outs, routes.T, prob.T, mib=8)
    return made[:3], made[3:]


def stage(residual, routes):
    return call(stage_kernel, of(TOK, D + LANES), residual, routes.T, mib=8)


def select(place, rows):
    outs = [of(QUAD, MAIN, WIDE)] * 2 + [of(2, QUAD, MAIN, WIDE)] * (FAR - 1)
    own, far, *pairs = call(select_kernel, outs, place, *rows, smem=1, mib=16)
    return own, far, pairs


def order(place, own, far, pairs, mate):
    scratch = [pltpu.VMEM((EXPERTS, MAIN, D), bf16), pltpu.VMEM((EXPERTS, MAIN, HALF), bf16)]
    args = (place, own, far, *pairs, mate)
    outs = of(SLOT_ROWS + REST_ROWS, D)
    return call(order_kernel, outs, *args, scratch=scratch, smem=1, mib=12)


def dispatch(attended, masks):
    outs = [of(TOK, MODEL), of(SLOT_ROWS, WIDE_MODEL)]
    return call(dispatch_kernel, outs, attended, *masks, mib=8)


def hidden_of(rows, residual, out_proj):
    return call(hidden_kernel, of(TOK, D, dtype=f32), rows, residual, out_proj, mib=12)


def experts(rows, residual, norm_gain, weights):
    scratch = [
        pltpu.VMEM((SLOT_ROWS + REST_ROWS, D), bf16),
        pltpu.VMEM((SLOT_ROWS + REST_ROWS, D), f32),
        *[pltpu.VMEM(w.shape, bf16) for w in weights],
        pltpu.SemaphoreType.DMA((5,)),
    ]
    args = (rows, residual, norm_gain.reshape(1, D), *weights)
    outs = of(SLOT_ROWS, WIDE)
    return call(expert_kernel, outs, *args, scratch=scratch, away=4, mib=50)


def mix(rows, hidden, probs):
    return call(mix_kernel, of(TOK, D), rows, hidden, *probs)


def exchange(x, axes):
    return lax.all_to_all(x, axes, split_axis=0, concat_axis=0, tiled=True)


def slots_exchange(x):
    return exchange(x.reshape(EXPERTS, MAIN, -1), ("y", "m")).reshape(SLOT_ROWS, -1)


def shift_pairs(j):
    pairs = []
    for y in range(RING):
        for m in range(QUAD):
            to = (y + (j if m & 1 else -j)) % RING
            pairs.append((y * QUAD + m, to * QUAD + m))
    return pairs


def layer(
    queries, keys, values, residual, out_proj, norm_gain, w_gate, w_up, w_down, routes, route_prob
):
    part = (lax.axis_index("ctx") % PARTS).astype(i32).reshape(1)
    place = jnp.stack([lax.axis_index("y"), lax.axis_index("m")]).astype(i32)
    packed = pack(queries, keys, values)
    gathered = exchange(packed, "ctx")
    mine = stage(residual, routes)
    beside = lax.ppermute(mine, "m", [(i, i ^ 2) for i in range(QUAD)])
    both = jnp.stack([mine, beside])
    others = lax.ppermute(both, "m", [(i, i ^ 1) for i in range(QUAD)])
    own, far, pairs = select(place, (mine, beside, others))
    far = lax.ppermute(far, "y", [(i, (i + FAR) % RING) for i in range(RING)])
    for j in range(1, FAR):
        pairs[j - 1] = lax.ppermute(pairs[j - 1], ("y", "m"), shift_pairs(j))
    masks, probs = plan(routes, route_prob)
    attended = attend(part, gathered)
    attended = exchange(attended, "ctx")
    rows, x = dispatch(attended, masks)
    x = slots_exchange(x)
    hidden = hidden_of(rows, residual, out_proj)
    mate = jnp.stack([pair[1] for pair in pairs])
    mate = lax.ppermute(mate, "m", [(i, i ^ 1) for i in range(QUAD)])
    ordered = order(place, own, far, pairs, mate)
    x = experts(x, ordered, norm_gain, (out_proj, w_gate, w_up, w_down))
    x = slots_exchange(x)
    return mix(x, hidden, probs)


def local(*args):
    args = [a if a.ndim < 3 else a[0] for a in args]
    return layer(*args)[None]


def solution(mesh):
    cut = Mesh(mesh.devices.reshape(N_CTX, RING, QUAD), ("ctx", "y", "m"))
    exp = ("y", "m")
    placed = (
        P(exp, "ctx", None),
        P(exp, "ctx", None),
        P(exp, "ctx", None),
        P(exp, "ctx", None),
        P(),
        P(),
        P(exp, None, None),
        P(exp, None, None),
        P(exp, None, None),
        P(exp, "ctx", None),
        P(exp, "ctx", None),
    )
    return jax.shard_map(
        local, mesh=cut, in_specs=placed, out_specs=P(exp, "ctx", None), check_vma=False
    )
```

```python
import jax
import jax.numpy as jnp
from jax import lax
from jax.experimental import pallas as pl
from jax.experimental.pallas import tpu as pltpu
from jax.sharding import Mesh
from jax.sharding import PartitionSpec as P

HEADS = 8
HEAD_DIM = 128
TOP = 4
TOK = 64
D = 2048
N_CTX = 24
EXPERTS = 32
PARTS = N_CTX // HEADS
Q_ROWS = 24
CHUNK = 2 * TOK + Q_ROWS
GROUP = 8
MAIN = 8
REST = 4
HALF = D // 2
WIDE = D + HALF
MODEL = HEADS * HEAD_DIM
HALF_MODEL = MODEL // 2
WIDE_MODEL = MODEL + HALF_MODEL
SLOT_ROWS = EXPERTS * MAIN
REST_ROWS = EXPERTS * REST
LANES = 128
RING = 8
QUAD = 4
FAR = 4
CODES = (0, 2, 1, 3)
f32 = jnp.float32
bf16 = jnp.bfloat16
i32 = jnp.int32


def dot(a, b):
    return jnp.dot(a, b, preferred_element_type=f32)


def dot_first(a, b):
    return lax.dot_general(a, b, (((0,), (0,)), ((), ())), preferred_element_type=f32)


def dot_last(a, b):
    return lax.dot_general(a, b, (((1,), (1,)), ((), ())), preferred_element_type=f32)


def part_rows(part):
    return min(Q_ROWS, TOK - part * Q_ROWS)


def pack_kernel(q_ref, k_ref, v_ref, o_ref):
    for head in range(HEADS):
        cols = slice(head * HEAD_DIM, (head + 1) * HEAD_DIM)
        for part in range(PARTS):
            rows = part_rows(part)
            chunk = head * PARTS + part
            o_ref[chunk, 0:TOK, :] = k_ref[:, cols]
            o_ref[chunk, TOK : 2 * TOK, :] = v_ref[:, cols]
            o_ref[chunk, 2 * TOK : 2 * TOK + rows, :] = q_ref[
                part * Q_ROWS : part * Q_ROWS + rows, cols
            ]
            if rows < Q_ROWS:
                o_ref[chunk, 2 * TOK + rows : CHUNK, :] = jnp.zeros((Q_ROWS - rows, HEAD_DIM), bf16)


def attend_kernel(part_ref, x_ref, o_ref):
    factor = HEAD_DIM ** (-0.5) * 1.4426950408889634
    rows = GROUP * Q_ROWS
    span = GROUP * TOK
    row = lax.broadcasted_iota(jnp.int32, (rows, span), 0)
    block = jnp.zeros((rows, span), jnp.int32)
    for b in range(1, GROUP):
        block = block + (row >= b * Q_ROWS).astype(jnp.int32)
    query_pos = row + block * (TOK - Q_ROWS) + part_ref[0] * Q_ROWS
    allowed = lax.broadcasted_iota(jnp.int32, (rows, span), 1) <= query_pos
    for g in range(N_CTX // GROUP):
        lo = g * GROUP
        hi = lo + GROUP
        queries = x_ref[lo:hi, 2 * TOK : CHUNK, :].reshape(rows, HEAD_DIM)
        near_keys = x_ref[lo:hi, 0:TOK, :].reshape(span, HEAD_DIM)
        near_values = x_ref[lo:hi, TOK : 2 * TOK, :].reshape(span, HEAD_DIM)
        near = jnp.where(allowed, dot_last(queries, near_keys), -1e30)
        top = jnp.max(near, axis=1, keepdims=True)
        if g:
            far_keys = x_ref[0:lo, 0:TOK, :].reshape(lo * TOK, HEAD_DIM)
            far_values = x_ref[0:lo, TOK : 2 * TOK, :].reshape(lo * TOK, HEAD_DIM)
            far = dot_last(queries, far_keys)
            top = jnp.maximum(top, jnp.max(far, axis=1, keepdims=True))
        near_exp = jnp.exp2((near - top) * factor)
        total = jnp.sum(near_exp, axis=1, keepdims=True)
        acc = dot(near_exp.astype(bf16), near_values)
        if g:
            far_exp = jnp.exp2((far - top) * factor)
            total = total + jnp.sum(far_exp, axis=1, keepdims=True)
            acc = acc + dot(far_exp.astype(bf16), far_values)
        o_ref[lo:hi] = (acc / total).astype(bf16).reshape(GROUP, Q_ROWS, HEAD_DIM)


def slots_of(routes):
    expert = lax.broadcasted_iota(i32, (EXPERTS, TOK), 0)
    named = jnp.zeros((EXPERTS, TOK), f32)
    for k in range(TOP):
        named = named + (routes[k : k + 1, :] == expert).astype(f32)
    earlier = (
        lax.broadcasted_iota(i32, (TOK, TOK), 0) < lax.broadcasted_iota(i32, (TOK, TOK), 1)
    ).astype(bf16)
    return named * (1.0 + dot(named.astype(bf16), earlier))


def masks_of(value):
    row = lax.broadcasted_iota(i32, value.shape, 0)
    main = value == ((row & 7) + 1).astype(f32)
    rest = value == ((row & 3) + 1 + MAIN).astype(f32)
    low = (row & 7) < REST
    return main, rest & low, rest & (~low)


def stage_kernel(residual_ref, routes_ref, o_ref):
    o_ref[:, 0:D] = residual_ref[...]
    row = lax.broadcasted_iota(i32, (TOK, EXPERTS), 0)
    expert = lax.broadcasted_iota(i32, (TOK, EXPERTS), 1)
    place = ((row >> 3) == (expert >> 2)) & ((row & 7) == (expert & 3))
    values = dot(place.astype(bf16), slots_of(routes_ref[...]).astype(bf16)).astype(bf16)
    o_ref[:, D : D + LANES] = jnp.concatenate([values, jnp.zeros((TOK, LANES - TOK), bf16)], axis=1)


def select_kernel(place_ref, *refs):
    m = place_ref[1]
    step = 2 * (m & 1) - 1
    row = lax.broadcasted_iota(i32, (TOK, TOK), 0) >> 3
    col = lax.broadcasted_iota(i32, (TOK, TOK), 1)
    other = row > FAR
    y = (place_ref[0] + step * jnp.where(other, row - FAR, row)) & (RING - 1)
    line = (col == y * 8 + jnp.where(other, m ^ 1, m)).astype(bf16)
    own_ref, far_ref, *pair_refs = refs[3:]
    mine_ref, beside_ref, others_ref = refs[:3]
    for source, rows_ref in enumerate((mine_ref, beside_ref, others_ref.at[0], others_ref.at[1])):
        value = dot(line, rows_ref[:, D : D + LANES])[:, 0:TOK]
        main, low, high = [mask.astype(bf16) for mask in masks_of(value)]
        whole = dot(main, rows_ref[:, 0:D]).astype(bf16)
        halves = (dot(low, rows_ref[:, 0:HALF]) + dot(high, rows_ref[:, HALF:D])).astype(bf16)
        for index in range(2 * FAR):
            part = slice(index * MAIN, (index + 1) * MAIN)
            if index == 0:
                out = own_ref.at[source]
            elif index == FAR:
                out = far_ref.at[source]
            else:
                out = pair_refs[index % FAR - 1].at[index // FAR, source]
            out[:, 0:D] = whole[part]
            out[:, D:WIDE] = halves[part]


def order_kernel(place_ref, own_ref, far_ref, *refs):
    pair_refs, (mate_ref, o_ref, main_ref, rest_ref) = refs[: FAR - 1], refs[FAR - 1 :]
    y, m = place_ref[0], place_ref[1]
    step = 2 * (m & 1) - 1

    def put(ref, index, away, flip):
        row = (y + away) & (RING - 1)
        for source in range(QUAD):
            target = row * QUAD + (m ^ flip ^ CODES[source])
            main_ref[target] = ref[(*index, source)][:, 0:D]
            rest_ref[target] = ref[(*index, source)][:, D:WIDE]

    put(own_ref, (), 0, 0)
    put(far_ref, (), FAR, 0)
    for j in range(1, FAR):
        put(pair_refs[j - 1], (0,), -step * j, 0)
        put(mate_ref, (j - 1,), step * j, 1)
    o_ref[0:SLOT_ROWS, :] = main_ref[...].reshape(SLOT_ROWS, D)
    halves = rest_ref[...].reshape(SLOT_ROWS, HALF)
    o_ref[SLOT_ROWS:, 0:HALF] = dot(picker(False), halves).astype(bf16)
    o_ref[SLOT_ROWS:, HALF:D] = dot(picker(True), halves).astype(bf16)


def plan_kernel(routes_ref, prob_ref, *outs):
    routes = routes_ref[...]
    expert = lax.broadcasted_iota(i32, (EXPERTS, TOK), 0)
    prob = jnp.zeros((EXPERTS, TOK), f32)
    for k in range(TOP):
        prob = prob + jnp.where(routes[k : k + 1, :] == expert, prob_ref[k : k + 1, :], 0.0)
    spread = (
        (lax.broadcasted_iota(i32, (SLOT_ROWS, EXPERTS), 0) >> 3)
        == lax.broadcasted_iota(i32, (SLOT_ROWS, EXPERTS), 1)
    ).astype(bf16)
    masks = masks_of(dot(spread, slots_of(routes).astype(bf16)))
    for mask, out in zip(masks, outs[:3]):
        out[...] = mask.astype(bf16)
    terms = []
    for _ in range(3):
        terms.append(prob.astype(bf16))
        prob = prob - terms[-1].astype(f32)
    wide = [dot(spread, term) for term in terms]
    for mask, out in zip(masks, outs[3:]):
        out[...] = jnp.concatenate([jnp.where(mask, w, 0.0) for w in wide], axis=1).astype(bf16)


def dispatch_kernel(a_ref, m_ref, l_ref, h_ref, rows_ref, o_ref):
    for head in range(HEADS):
        cols = slice(head * HEAD_DIM, (head + 1) * HEAD_DIM)
        for part in range(PARTS):
            rows = part_rows(part)
            rows_ref[part * Q_ROWS : part * Q_ROWS + rows, cols] = a_ref[
                head * PARTS + part, 0:rows, :
            ]
    o_ref[:, 0:MODEL] = dot(m_ref[...], rows_ref[...]).astype(bf16)
    o_ref[:, MODEL:WIDE_MODEL] = (
        dot(l_ref[...], rows_ref[:, 0:HALF_MODEL]) + dot(h_ref[...], rows_ref[:, HALF_MODEL:MODEL])
    ).astype(bf16)


def hidden_kernel(rows_ref, residual_ref, w_ref, o_ref):
    o_ref[...] = residual_ref[...].astype(f32) + dot(rows_ref[...], w_ref[...])


def picker(high):
    row = lax.broadcasted_iota(jnp.int32, (REST_ROWS, SLOT_ROWS), 0)
    col = lax.broadcasted_iota(jnp.int32, (REST_ROWS, SLOT_ROWS), 1)
    return (col == (row >> 2) * MAIN + (row & 3) + (REST if high else 0)).astype(bf16)


def expert_kernel(x_ref, residual_ref, gain_ref, *refs):
    weights, (o_ref, rows_ref, hidden_ref, w_ref, gate_ref, up_ref, down_ref, sems) = refs[:4], refs[4:]
    halves = (slice(0, HALF), slice(HALF, D))
    pairs = [(weights[0].at[:, cols], w_ref.at[:, cols]) for cols in halves]
    pairs += list(zip(weights[1:3], (gate_ref, up_ref)))
    pairs += [(weights[3].at[:, cols], down_ref.at[:, cols]) for cols in halves]
    copies = [
        pltpu.make_async_copy(source, target, sems.at[i])
        for i, (source, target) in enumerate(pairs)
    ]
    for copy in copies:
        copy.start()
    low, high = picker(False), picker(True)
    main = slice(0, SLOT_ROWS)
    rest = slice(SLOT_ROWS, SLOT_ROWS + REST_ROWS)
    tail = x_ref[:, MODEL:WIDE_MODEL]
    tail = jnp.concatenate([dot(low, tail), dot(high, tail)], axis=1).astype(bf16)
    attended = ((main, x_ref[:, 0:MODEL]), (rest, tail))
    squares = [0.0, 0.0]
    for copy, cols in zip(copies, halves):
        copy.wait()
        for i, (rows, have) in enumerate(attended):
            hidden = residual_ref[rows, cols].astype(f32) + dot(have, w_ref[:, cols])
            squares[i] += jnp.sum(hidden * hidden, axis=-1, keepdims=True)
            hidden_ref[rows, cols] = hidden
    for (rows, _), square in zip(attended, squares):
        factor = lax.rsqrt(square * (1.0 / D) + 1e-05)
        rows_ref[rows, :] = (hidden_ref[rows, :] * factor * gain_ref[...]).astype(bf16)
    copies[2].wait()
    gate = dot(rows_ref[...], gate_ref[...])
    copies[3].wait()
    up = dot(rows_ref[...], up_ref[...])
    act = (gate / (1.0 + jnp.exp(-gate)) * up).astype(bf16)
    made = []
    for copy, cols in zip(copies[4:], halves):
        copy.wait()
        made.append(dot(act, down_ref[:, cols]).astype(bf16))
        o_ref[:, cols] = made[-1][main]
    o_ref[:, D:WIDE] = (dot_first(low, made[0][rest]) + dot_first(high, made[1][rest])).astype(bf16)


def mix_kernel(y_ref, hidden_ref, m_ref, l_ref, h_ref, o_ref):
    def terms(p_ref, rows):
        made = dot_first(p_ref[...], rows)
        return made[0:TOK] + made[TOK : 2 * TOK] + made[2 * TOK :]

    total = hidden_ref[...] + terms(m_ref, y_ref[:, 0:D])
    rest = y_ref[:, D:WIDE]
    o_ref[:, 0:HALF] = (total[:, 0:HALF] + terms(l_ref, rest)).astype(bf16)
    o_ref[:, HALF:D] = (total[:, HALF:D] + terms(h_ref, rest)).astype(bf16)


def call(kernel, outs, *args, scratch=(), smem=0, away=0, mib=16):
    vmem = pl.BlockSpec(memory_space=pltpu.VMEM)
    specs = [pl.BlockSpec(memory_space=pltpu.SMEM)] * smem + [vmem] * (len(args) - smem - away)
    many = isinstance(outs, list)
    return pl.pallas_call(
        kernel,
        out_shape=outs,
        in_specs=specs + [pl.BlockSpec(memory_space=pltpu.HBM)] * away,
        out_specs=[vmem] * len(outs) if many else vmem,
        scratch_shapes=scratch,
        compiler_params=pltpu.CompilerParams(vmem_limit_bytes=mib * 1024 * 1024),
    )(*args)


def of(*dims, dtype=bf16):
    return jax.ShapeDtypeStruct(dims, dtype)


def pack(queries, keys, values):
    return call(pack_kernel, of(N_CTX, CHUNK, HEAD_DIM), queries, keys, values, mib=56)


def attend(part, gathered):
    return call(attend_kernel, of(N_CTX, Q_ROWS, HEAD_DIM), part, gathered, smem=1)


def plan(routes, prob):
    outs = [of(SLOT_ROWS, TOK)] * 3 + [of(SLOT_ROWS, 3 * TOK)] * 3
    made = call(plan_kernel, outs, routes.T, prob.T, mib=8)
    return made[:3], made[3:]


def stage(residual, routes):
    return call(stage_kernel, of(TOK, D + LANES), residual, routes.T, mib=8)


def select(place, rows):
    outs = [of(QUAD, MAIN, WIDE)] * 2 + [of(2, QUAD, MAIN, WIDE)] * (FAR - 1)
    own, far, *pairs = call(select_kernel, outs, place, *rows, smem=1, mib=16)
    return own, far, pairs


def order(place, own, far, pairs, mate):
    scratch = [pltpu.VMEM((EXPERTS, MAIN, D), bf16), pltpu.VMEM((EXPERTS, MAIN, HALF), bf16)]
    args = (place, own, far, *pairs, mate)
    outs = of(SLOT_ROWS + REST_ROWS, D)
    return call(order_kernel, outs, *args, scratch=scratch, smem=1, mib=12)


def dispatch(attended, masks):
    outs = [of(TOK, MODEL), of(SLOT_ROWS, WIDE_MODEL)]
    return call(dispatch_kernel, outs, attended, *masks, mib=8)


def hidden_of(rows, residual, out_proj):
    return call(hidden_kernel, of(TOK, D, dtype=f32), rows, residual, out_proj, mib=12)


def experts(rows, residual, norm_gain, weights):
    scratch = [
        pltpu.VMEM((SLOT_ROWS + REST_ROWS, D), bf16),
        pltpu.VMEM((SLOT_ROWS + REST_ROWS, D), f32),
        *[pltpu.VMEM(w.shape, bf16) for w in weights],
        pltpu.SemaphoreType.DMA((6,)),
    ]
    args = (rows, residual, norm_gain.reshape(1, D), *weights)
    outs = of(SLOT_ROWS, WIDE)
    return call(expert_kernel, outs, *args, scratch=scratch, away=4, mib=50)


def mix(rows, hidden, probs):
    return call(mix_kernel, of(TOK, D), rows, hidden, *probs)


def exchange(x, axes):
    return lax.all_to_all(x, axes, split_axis=0, concat_axis=0, tiled=True)


def slots_exchange(x):
    return exchange(x.reshape(EXPERTS, MAIN, -1), ("y", "m")).reshape(SLOT_ROWS, -1)


def shift_pairs(j):
    pairs = []
    for y in range(RING):
        for m in range(QUAD):
            to = (y + (j if m & 1 else -j)) % RING
            pairs.append((y * QUAD + m, to * QUAD + m))
    return pairs


def layer(
    queries, keys, values, residual, out_proj, norm_gain, w_gate, w_up, w_down, routes, route_prob
):
    part = (lax.axis_index("ctx") % PARTS).astype(i32).reshape(1)
    place = jnp.stack([lax.axis_index("y"), lax.axis_index("m")]).astype(i32)
    packed = pack(queries, keys, values)
    gathered = exchange(packed, "ctx")
    mine = stage(residual, routes)
    beside = lax.ppermute(mine, "m", [(i, i ^ 2) for i in range(QUAD)])
    both = jnp.stack([mine, beside])
    others = lax.ppermute(both, "m", [(i, i ^ 1) for i in range(QUAD)])
    own, far, pairs = select(place, (mine, beside, others))
    far = lax.ppermute(far, "y", [(i, (i + FAR) % RING) for i in range(RING)])
    for j in range(1, FAR):
        pairs[j - 1] = lax.ppermute(pairs[j - 1], ("y", "m"), shift_pairs(j))
    masks, probs = plan(routes, route_prob)
    attended = attend(part, gathered)
    attended = exchange(attended, "ctx")
    rows, x = dispatch(attended, masks)
    x = slots_exchange(x)
    hidden = hidden_of(rows, residual, out_proj)
    mate = jnp.stack([pair[1] for pair in pairs])
    mate = lax.ppermute(mate, "m", [(i, i ^ 1) for i in range(QUAD)])
    ordered = order(place, own, far, pairs, mate)
    x = experts(x, ordered, norm_gain, (out_proj, w_gate, w_up, w_down))
    x = slots_exchange(x)
    return mix(x, hidden, probs)


def local(*args):
    args = [a if a.ndim < 3 else a[0] for a in args]
    return layer(*args)[None]


def solution(mesh):
    cut = Mesh(mesh.devices.reshape(N_CTX, RING, QUAD), ("ctx", "y", "m"))
    exp = ("y", "m")
    placed = (
        P(exp, "ctx", None),
        P(exp, "ctx", None),
        P(exp, "ctx", None),
        P(exp, "ctx", None),
        P(),
        P(),
        P(exp, None, None),
        P(exp, None, None),
        P(exp, None, None),
        P(exp, "ctx", None),
        P(exp, "ctx", None),
    )
    return jax.shard_map(
        local, mesh=cut, in_specs=placed, out_specs=P(exp, "ctx", None), check_vma=False
    )
```
